32 devices in a mesh: head: 4 (over y, x), shard: 8 (over z, core).
Axes of the slice: x: 2, y: 2, z: 4, core: 2. Of those that a mesh axis runs over, the one named last changes fastest.
Arguments:
- tokens: bfloat16 [4, 1024, 640], P('head', 'shard'), may hold values from -6 to 6
- attn_norm: bfloat16 [640], P('shard'), may hold values from 0.099609375 to 1.8984375
- query_norm: bfloat16 [256], P('shard'), may hold values from 0.099609375 to 1.8984375
- key_norm: bfloat16 [256], P('shard'), may hold values from 0.099609375 to 1.8984375
- post_attn_norm: bfloat16 [640], P('shard'), may hold values from 0.099609375 to 1.8984375
- ffn_norm: bfloat16 [640], P('shard'), may hold values from 0.099609375 to 1.8984375
- post_ffn_norm: bfloat16 [640], P('shard'), may hold values from 0.099609375 to 1.8984375
- query_weight: bfloat16 [640, 1024], P(None, 'shard'), may hold values from -0.25 to 0.25
- keyval_weight: bfloat16 [640, 512], P(None, 'shard'), may hold values from -0.25 to 0.25
- out_weight: bfloat16 [1024, 640], P('shard'), may hold values from -0.375 to 0.375
- gate_weight: bfloat16 [640, 2048], P(None, 'shard'), may hold values from -0.25 to 0.25
- up_weight: bfloat16 [640, 2048], P(None, 'shard'), may hold values from -0.25 to 0.25
- down_weight: bfloat16 [2048, 640], P('shard'), may hold values from -0.125 to 0.125
- cotangent: float32 [4, 1024, 640], P('head', 'shard'), may hold values from -6 to 6
Outputs:
- output: float32 [4, 1024, 640], P('head', 'shard')
- tokens_grad: float32 [4, 1024, 640], P('head', 'shard')
- attn_norm_grad: float32 [640], P('shard')
- query_norm_grad: float32 [256], P('shard')
- key_norm_grad: float32 [256], P('shard')
- post_attn_grad: float32 [640], P('shard')
- ffn_norm_grad: float32 [640], P('shard')
- post_ffn_grad: float32 [640], P('shard')
- query_weight_grad: float32 [640, 1024], P(None, 'shard')
- keyval_weight_grad: float32 [640, 512], P(None, 'shard')
- out_weight_grad: float32 [1024, 640], P('shard')
- gate_weight_grad: float32 [640, 2048], P(None, 'shard')
- up_weight_grad: float32 [640, 2048], P(None, 'shard')
- down_weight_grad: float32 [2048, 640], P('shard')
The draws below stay inside these ranges and needn't reach their ends.
All inputs are finite; a program needn't handle non-finite values.
Results may differ from the reference program's by a relative error of at most 0.023.
Values may be sent and summed in bfloat16 or wider, within the bound.
No kernel may reach another device: no remote copies, remote signals or barrier semaphores. Data moves between devices by JAX's collectives and lax.ppermute only.
A program may use at most 256 MiB of HBM per device.

```python
import math
import jax
import jax.numpy as jnp
from jax import lax

D = 640
HEADS = 4
HD = 256
FF = 2048
SEQS = 4
LEN = 1024


def block_scale(own_key, shape, cuts, low, high):
    factor_of = 1.0
    for axis_at, shards_of in cuts:
        draws = jax.random.uniform(jax.random.fold_in(jax.random.fold_in(own_key, 6), axis_at), (shards_of,), jnp.float32, low / len(cuts), high / len(cuts))
        factor_of = factor_of * jnp.repeat(jnp.exp(draws), shape[axis_at] // shards_of).reshape((-1,) + (1,) * (len(shape) - 1 - axis_at))
    return factor_of


def noise(stream_key, extent, scale, bound, shards=(), kind=jnp.bfloat16):
    factor_of = block_scale(stream_key, extent, shards, -0.22, 0.18) if shards else 1.0
    entries = jax.random.normal(stream_key, extent, jnp.float32) * scale * factor_of
    return jnp.minimum(jnp.maximum(entries, -bound), bound).astype(kind)


def setup_inputs(seed: int = 0) -> dict:
    splits = jax.random.split(jax.random.key(seed), 15)
    return {
        "tokens": noise(splits[0], (SEQS, LEN, D), 1.0, 6.0, ((0, 4), (1, 8))),
        "attn_norm": jnp.clip(1.0 + 0.18 * jax.random.normal(splits[1], (D,), jnp.float32), 0.099609375, 1.8984375).astype(jnp.bfloat16),
        "query_norm": jnp.clip(1.0 + 0.18 * jax.random.normal(splits[2], (HD,), jnp.float32), 0.099609375, 1.8984375).astype(jnp.bfloat16),
        "key_norm": jnp.clip(1.0 + 0.18 * jax.random.normal(splits[3], (HD,), jnp.float32), 0.099609375, 1.8984375).astype(jnp.bfloat16),
        "post_attn_norm": jnp.clip(1.0 + 0.18 * jax.random.normal(splits[4], (D,), jnp.float32), 0.099609375, 1.8984375).astype(jnp.bfloat16),
        "ffn_norm": jnp.clip(1.0 + 0.18 * jax.random.normal(splits[5], (D,), jnp.float32), 0.099609375, 1.8984375).astype(jnp.bfloat16),
        "post_ffn_norm": jnp.clip(1.0 + 0.18 * jax.random.normal(splits[6], (D,), jnp.float32), 0.099609375, 1.8984375).astype(jnp.bfloat16),
        "query_weight": noise(splits[7], (D, HEADS * HD), D ** -0.5, 0.25, ((1, 8),)),
        "keyval_weight": noise(splits[8], (D, 2 * HD), D ** -0.5, 0.25, ((1, 8),)),
        "out_weight": noise(splits[9], (HEADS * HD, D), HD ** -0.5, 0.375, ((0, 8),)),
        "gate_weight": noise(splits[10], (D, FF), D ** -0.5, 0.25, ((1, 8),)),
        "up_weight": noise(splits[11], (D, FF), D ** -0.5, 0.25, ((1, 8),)),
        "down_weight": noise(splits[12], (FF, D), FF ** -0.5, 0.125, ((0, 8),)),
        "cotangent": noise(splits[13], (SEQS, LEN, D), 1.0, 6.0, ((0, 4), (1, 8)), jnp.float32),
    }


norm_eps = 1e-06
rope_base = 1000000.0
score_scale = 0.0625
gelu_coef = 0.7978845608028654

def rms_scale(values):
    return lax.rsqrt(lax.optimization_barrier(jnp.mean(values * values, axis=-1, keepdims=True)) + norm_eps)

def norm_back(upstream, values, gain):
    scale = rms_scale(values)
    weighted = upstream * gain
    inner = lax.optimization_barrier(jnp.mean(weighted * values, axis=-1, keepdims=True))
    grad_values = scale * weighted - values * (scale * scale * scale) * inner
    leading = tuple(range(values.ndim - 1))
    grad_gain = lax.optimization_barrier(jnp.sum(upstream * values * scale, axis=leading))
    return (grad_values, grad_gain)

def rotate(values, positions, direction):
    half = values.shape[-1] // 2
    index = jnp.arange(half, dtype=jnp.float32)
    freqs = jnp.exp(index * (-2.0 * math.log(rope_base) / values.shape[-1]))
    angles = positions.astype(jnp.float32)[..., None] * freqs
    cosine = jnp.cos(angles)
    sine = direction * jnp.sin(angles)
    first = values[..., :half]
    second = values[..., half:]
    return jnp.concatenate([first * cosine - second * sine, second * cosine + first * sine], axis=-1)

def gelu_parts(values):
    inner = gelu_coef * (values + 0.044715 * values * values * values)
    tanh_value = jnp.tanh(inner)
    value = 0.5 * values * (1.0 + tanh_value)
    slope = 0.5 * (1.0 + tanh_value) + 0.5 * values * (1.0 - tanh_value * tanh_value) * gelu_coef * (1.0 + 3.0 * 0.044715 * values * values)
    return (value, slope)

def contract_rows(left, right):
    return lax.dot_general(left, right, (((0,), (0,)), ((), ())), preferred_element_type=jnp.float32)

def contract_cols(left, right):
    return lax.dot_general(left, right, (((1,), (1,)), ((), ())), preferred_element_type=jnp.float32)

def one_sequence(seq_tokens, seq_cot, gains, mats):
    gain_attn, gain_query, gain_key, gain_post_attn, gain_ffn, gain_post_ffn = gains
    query_weight, keyval_weight, out_weight, gate_weight, up_weight, down_weight = mats
    length = seq_tokens.shape[0]
    heads = query_weight.shape[1] // key_width_of(keyval_weight)
    width = key_width_of(keyval_weight)
    positions = jnp.arange(length, dtype=jnp.int32)
    residual_in = seq_tokens.astype(jnp.float32)
    normed_in = (residual_in * rms_scale(residual_in) * gain_attn).astype(jnp.bfloat16)
    query_raw = jnp.dot(normed_in, query_weight, preferred_element_type=jnp.float32).reshape(length, heads, width)
    keyval_raw = jnp.dot(normed_in, keyval_weight, preferred_element_type=jnp.float32)
    key_raw = keyval_raw[:, :width]
    query_rot = rotate(query_raw * rms_scale(query_raw) * gain_query, positions[:, None], 1.0).astype(jnp.bfloat16)
    key_rot = rotate(key_raw * rms_scale(key_raw) * gain_key, positions, 1.0).astype(jnp.bfloat16)
    value_rot = keyval_raw[:, width:].astype(jnp.bfloat16)
    key_wide = key_rot.astype(jnp.float32)
    value_wide = value_rot.astype(jnp.float32)
    block = math.gcd(length, 1024)
    number = length // block
    starts = jnp.arange(number, dtype=jnp.int32) * block
    query_blocks = query_rot.reshape(number, block, heads, width)

    def block_scores(query_block, start):
        scores = jnp.einsum('ihd,jd->hij', query_block.astype(jnp.float32), key_wide) * score_scale
        query_pos = start + jnp.arange(block, dtype=jnp.int32)
        allowed = query_pos[:, None] >= positions[None, :]
        return jnp.where(allowed[None], scores, -1e+30)

    def attend_block(pair):
        query_block, start = pair
        scores = block_scores(query_block, start)
        top = lax.optimization_barrier(jnp.max(scores, axis=-1, keepdims=True))
        log_norm = top + jnp.log(lax.optimization_barrier(jnp.sum(jnp.exp(scores - top), axis=-1, keepdims=True)))
        probs = jnp.exp(scores - log_norm).astype(jnp.bfloat16)
        mixed = jnp.einsum('hij,jd->ihd', probs.astype(jnp.float32), value_wide).astype(jnp.bfloat16)
        return (mixed, log_norm[..., 0])
    attended_blocks, log_norms = lax.map(attend_block, (query_blocks, starts))
    attended = attended_blocks.reshape(length, heads * width)
    attn_raw = jnp.dot(attended, out_weight, preferred_element_type=jnp.float32)
    residual_mid = residual_in + attn_raw * rms_scale(attn_raw) * gain_post_attn
    normed_mid = (residual_mid * rms_scale(residual_mid) * gain_ffn).astype(jnp.bfloat16)
    gate_raw = jnp.dot(normed_mid, gate_weight, preferred_element_type=jnp.float32)
    up_raw = jnp.dot(normed_mid, up_weight, preferred_element_type=jnp.float32)
    gelu_value, gelu_slope = gelu_parts(gate_raw)
    hidden = (gelu_value * up_raw).astype(jnp.bfloat16)
    ffn_raw = jnp.dot(hidden, down_weight, preferred_element_type=jnp.float32)
    output = residual_mid + ffn_raw * rms_scale(ffn_raw) * gain_post_ffn
    grad_ffn_raw, grad_post_ffn = norm_back(seq_cot, ffn_raw, gain_post_ffn)
    grad_ffn_b = grad_ffn_raw.astype(jnp.bfloat16)
    grad_down = contract_rows(hidden, grad_ffn_b)
    grad_hidden = contract_cols(grad_ffn_b, down_weight)
    grad_gate_b = (grad_hidden * up_raw * gelu_slope).astype(jnp.bfloat16)
    grad_up_b = (grad_hidden * gelu_value).astype(jnp.bfloat16)
    grad_gate = contract_rows(normed_mid, grad_gate_b)
    grad_up = contract_rows(normed_mid, grad_up_b)
    grad_normed_mid = contract_cols(grad_gate_b, gate_weight) + contract_cols(grad_up_b, up_weight)
    grad_mid_part, grad_ffn_gain = norm_back(grad_normed_mid, residual_mid, gain_ffn)
    grad_mid = seq_cot + grad_mid_part
    grad_attn_raw, grad_post_attn = norm_back(grad_mid, attn_raw, gain_post_attn)
    grad_attn_b = grad_attn_raw.astype(jnp.bfloat16)
    grad_out = contract_rows(attended, grad_attn_b)
    attended_grad = contract_cols(grad_attn_b, out_weight).astype(jnp.bfloat16).reshape(number, block, heads, width)

    def back_block(carry, items):
        key_sum, value_sum = carry
        query_block, grad_block, mixed_block, log_block, start = items
        scores = block_scores(query_block, start)
        probs = jnp.exp(scores - log_block[..., None])
        delta = lax.optimization_barrier(jnp.sum(grad_block.astype(jnp.float32) * mixed_block.astype(jnp.float32), axis=-1))
        prob_grad = jnp.einsum('ihd,jd->hij', grad_block.astype(jnp.float32), value_wide)
        score_grad = (probs * (prob_grad - jnp.transpose(delta)[..., None])).astype(jnp.bfloat16).astype(jnp.float32)
        query_part = jnp.einsum('hij,jd->ihd', score_grad, key_wide) * score_scale
        key_sum = key_sum + jnp.einsum('hij,ihd->jd', score_grad, query_block.astype(jnp.float32)) * score_scale
        value_sum = value_sum + jnp.einsum('hij,ihd->jd', probs.astype(jnp.bfloat16).astype(jnp.float32), grad_block.astype(jnp.float32))
        return ((key_sum, value_sum), query_part)
    empty = jnp.zeros((length, width), jnp.float32)
    (key_grad, value_grad), query_parts = lax.scan(back_block, (empty, empty), (query_blocks, attended_grad, attended_blocks, log_norms, starts))
    query_grad = query_parts.reshape(length, heads, width)
    grad_query_raw, grad_query_gain = norm_back(rotate(query_grad, positions[:, None], -1.0), query_raw, gain_query)
    grad_key_raw, grad_key_gain = norm_back(rotate(key_grad, positions, -1.0), key_raw, gain_key)
    grad_query_b = grad_query_raw.reshape(length, heads * width).astype(jnp.bfloat16)
    grad_keyval_b = jnp.concatenate([grad_key_raw, value_grad], axis=-1).astype(jnp.bfloat16)
    grad_query_w = contract_rows(normed_in, grad_query_b)
    grad_keyval_w = contract_rows(normed_in, grad_keyval_b)
    grad_normed_in = contract_cols(grad_query_b, query_weight) + contract_cols(grad_keyval_b, keyval_weight)
    grad_in_part, grad_attn_gain = norm_back(grad_normed_in, residual_in, gain_attn)
    tokens_grad = grad_mid + grad_in_part
    grads = (grad_attn_gain, grad_query_gain, grad_key_gain, grad_post_attn, grad_ffn_gain, grad_post_ffn, grad_query_w, grad_keyval_w, grad_out, grad_gate, grad_up, grad_down)
    return (output, tokens_grad, grads)

def key_width_of(keyval_weight):
    return keyval_weight.shape[1] // 2

def reference(tokens, attn_norm, query_norm, key_norm, post_attn_norm, ffn_norm, post_ffn_norm, query_weight, keyval_weight, out_weight, gate_weight, up_weight, down_weight, cotangent):
    gains = tuple((g.astype(jnp.float32) for g in (attn_norm, query_norm, key_norm, post_attn_norm, ffn_norm, post_ffn_norm)))
    mats = (query_weight, keyval_weight, out_weight, gate_weight, up_weight, down_weight)
    start_totals = tuple((jnp.zeros(p.shape, jnp.float32) for p in gains + mats))

    def per_sequence(totals, items):
        seq_tokens, seq_cot = items
        output, tokens_grad, grads = one_sequence(seq_tokens, seq_cot, gains, mats)
        return (jax.tree.map(jnp.add, totals, grads), (output, tokens_grad))
    totals, (output, tokens_grad) = lax.scan(per_sequence, start_totals, (tokens, cotangent))
    return (output, tokens_grad, totals[0], totals[1], totals[2], totals[3], totals[4], totals[5], totals[6], totals[7], totals[8], totals[9], totals[10], totals[11])
```

```python
import functools
import math

import jax
import jax.numpy as jnp
from jax import lax
from jax.experimental import pallas as pl
from jax.experimental.pallas import tpu as pltpu
from jax.sharding import PartitionSpec as P

HEADS = 4
HD = 256


norm_eps = 1e-06
rope_base = 1000000.0
score_scale = 0.0625
gelu_coef = 0.7978845608028654


def rms_scale(values):
    return lax.rsqrt(jnp.mean(values * values, axis=-1, keepdims=True) + norm_eps)


def norm_back(upstream, values, gain):
    scale = rms_scale(values)
    weighted = upstream * gain
    inner = jnp.mean(weighted * values, axis=-1, keepdims=True)
    grad_values = scale * weighted - values * (scale * scale * scale) * inner
    leading = tuple(range(values.ndim - 1))
    grad_gain = jnp.sum(upstream * values * scale, axis=leading)
    return (grad_values, grad_gain)


def rotate(values, positions, direction):
    half = values.shape[-1] // 2
    index = jnp.arange(half, dtype=jnp.float32)
    freqs = jnp.exp(index * (-2.0 * math.log(rope_base) / values.shape[-1]))
    angles = positions.astype(jnp.float32)[..., None] * freqs
    cosine = jnp.cos(angles)
    sine = direction * jnp.sin(angles)
    first = values[..., :half]
    second = values[..., half:]
    return jnp.concatenate(
        [first * cosine - second * sine, second * cosine + first * sine], axis=-1
    )


def gelu_parts(values):
    inner = gelu_coef * (values + 0.044715 * values * values * values)
    tanh_value = jnp.tanh(inner)
    value = 0.5 * values * (1.0 + tanh_value)
    slope = 0.5 * (1.0 + tanh_value) + 0.5 * values * (
        1.0 - tanh_value * tanh_value
    ) * gelu_coef * (1.0 + 3.0 * 0.044715 * values * values)
    return (value, slope)


def contract_rows(left, right):
    return lax.dot_general(
        left, right, (((0,), (0,)), ((), ())), preferred_element_type=jnp.float32
    )


def contract_cols(left, right):
    return lax.dot_general(
        left, right, (((1,), (1,)), ((), ())), preferred_element_type=jnp.float32
    )


def masked_scores(queries, keys, query_pos, key_start):
    scores = (
        jnp.einsum("gid,gjd->gij", queries, keys, preferred_element_type=jnp.float32) * score_scale
    )
    key_pos = key_start + jnp.arange(keys.shape[1], dtype=jnp.int32)
    allowed = query_pos[:, None] >= key_pos[None, :]
    return (jnp.where(allowed[None], scores, -1e30), allowed)


def sweep_tiles(visit, state, piece, last_pos):
    count = piece.shape[1]
    tile = math.gcd(count, 2048)
    number = count // tile

    def sweep_step_tile(index, current):
        offset = index * tile
        tile_data = lax.dynamic_slice_in_dim(piece, index * tile, tile, 1)
        return lax.cond(
            offset <= last_pos,
            lambda held: visit(held, tile_data, offset),
            lambda held: held,
            current,
        )

    return lax.fori_loop(0, number, sweep_step_tile, state)


def body(
    tokens,
    attn_norm,
    query_norm,
    key_norm,
    post_attn_norm,
    ffn_norm,
    post_ffn_norm,
    query_weight,
    keyval_weight,
    out_weight,
    gate_weight,
    up_weight,
    down_weight,
    cotangent,
):
    gathered = (
        lax.all_gather(attn_norm, "shard", axis=0, tiled=True),
        lax.all_gather(query_norm, "shard", axis=0, tiled=True),
        lax.all_gather(key_norm, "shard", axis=0, tiled=True),
        lax.all_gather(post_attn_norm, "shard", axis=0, tiled=True),
        lax.all_gather(ffn_norm, "shard", axis=0, tiled=True),
        lax.all_gather(post_ffn_norm, "shard", axis=0, tiled=True),
        lax.all_gather(query_weight, "shard", axis=1, tiled=True),
        lax.all_gather(keyval_weight, "shard", axis=1, tiled=True),
        lax.all_gather(out_weight, "shard", axis=0, tiled=True),
        lax.all_gather(gate_weight, "shard", axis=1, tiled=True),
        lax.all_gather(up_weight, "shard", axis=1, tiled=True),
        lax.all_gather(down_weight, "shard", axis=0, tiled=True),
    )
    gain_attn, gain_query, gain_key, gain_post_attn, gain_ffn, gain_post_ffn = [
        g.astype(jnp.float32) for g in gathered[:6]
    ]
    full_query, full_keyval, full_out, full_gate, full_up, full_down = gathered[6:]
    back_query, back_keyval, back_out, back_gate, back_up, back_down = gathered[6:]
    rows = tokens.shape[1]
    positions = lax.axis_index("shard") * rows + jnp.arange(rows, dtype=jnp.int32)
    first_pos = positions[0]
    last_pos = positions[rows - 1]
    residual_in = tokens[0].astype(jnp.float32)
    normed_in = (residual_in * rms_scale(residual_in) * gain_attn).astype(jnp.bfloat16)
    query_raw = jnp.dot(normed_in, full_query, preferred_element_type=jnp.float32).reshape(
        rows, HEADS, HD
    )
    keyval_raw = jnp.dot(normed_in, full_keyval, preferred_element_type=jnp.float32)
    key_raw = keyval_raw[:, :HD]
    query_rot = rotate(
        query_raw * rms_scale(query_raw) * gain_query, positions[:, None], 1.0
    ).astype(jnp.bfloat16)
    key_rot = rotate(key_raw * rms_scale(key_raw) * gain_key, positions, 1.0).astype(jnp.bfloat16)
    keyval_rot = jnp.concatenate([key_rot, keyval_raw[:, HD:].astype(jnp.bfloat16)], axis=-1)
    query_heads_first = jnp.transpose(query_rot, (1, 0, 2))
    keyval_copies = jnp.broadcast_to(keyval_rot[None], (HEADS, rows, 2 * HD))
    head_queries, head_keyvals = (
        lax.all_to_all(query_heads_first, "head", split_axis=0, concat_axis=0, tiled=True),
        lax.all_to_all(keyval_copies, "head", split_axis=0, concat_axis=0, tiled=True),
    )
    seq_count = head_queries.shape[0]

    def online_tile(state, tile_data, offset):
        running_max, running_sum, weighted = state
        scores, allowed = masked_scores(head_queries, tile_data[:, :, :HD], positions, offset)
        new_max = jnp.maximum(running_max, jnp.max(scores, axis=-1))
        probs = jnp.where(allowed[None], jnp.exp(scores - new_max[..., None]), 0.0)
        fade = jnp.exp(running_max - new_max)
        running_sum = running_sum * fade + jnp.sum(probs, axis=-1)
        weighted = weighted * fade[..., None] + jnp.einsum(
            "gij,gjd->gid",
            probs.astype(jnp.bfloat16),
            tile_data[:, :, HD:],
            preferred_element_type=jnp.float32,
        )
        return (new_max, running_sum, weighted)

    start_state = (
        jnp.full((seq_count, rows), -1e30, jnp.float32),
        jnp.zeros((seq_count, rows), jnp.float32),
        jnp.zeros((seq_count, rows, HD), jnp.float32),
    )
    all_keyvals = lax.all_gather(head_keyvals, "shard", axis=1, tiled=True)
    final_state = sweep_tiles(online_tile, start_state, all_keyvals, last_pos)
    top_score, total_weight, weighted_sum = final_state
    attended = (weighted_sum / total_weight[..., None]).astype(jnp.bfloat16)
    log_norm = top_score + jnp.log(total_weight)
    returned = lax.all_to_all(attended, "head", split_axis=0, concat_axis=0, tiled=True)
    own_heads = jnp.transpose(returned, (1, 0, 2)).reshape(rows, HEADS * HD)
    attn_raw = jnp.dot(own_heads, full_out, preferred_element_type=jnp.float32)
    residual_mid = residual_in + attn_raw * rms_scale(attn_raw) * gain_post_attn
    normed_mid = (residual_mid * rms_scale(residual_mid) * gain_ffn).astype(jnp.bfloat16)
    gate_raw = jnp.dot(normed_mid, full_gate, preferred_element_type=jnp.float32)
    up_raw = jnp.dot(normed_mid, full_up, preferred_element_type=jnp.float32)
    gelu_value, gelu_slope = gelu_parts(gate_raw)
    hidden = (gelu_value * up_raw).astype(jnp.bfloat16)
    ffn_raw = jnp.dot(hidden, full_down, preferred_element_type=jnp.float32)
    result = residual_mid + ffn_raw * rms_scale(ffn_raw) * gain_post_ffn
    upstream = cotangent[0]
    grad_ffn_raw, grad_post_ffn = norm_back(upstream, ffn_raw, gain_post_ffn)
    grad_ffn_b = grad_ffn_raw.astype(jnp.bfloat16)
    grad_down = contract_rows(hidden, grad_ffn_b)
    grad_hidden = contract_cols(grad_ffn_b, back_down)
    grad_gate_b = (grad_hidden * up_raw * gelu_slope).astype(jnp.bfloat16)
    grad_up_b = (grad_hidden * gelu_value).astype(jnp.bfloat16)
    grad_gate = contract_rows(normed_mid, grad_gate_b)
    grad_up = contract_rows(normed_mid, grad_up_b)
    grad_normed_mid = contract_cols(grad_gate_b, back_gate) + contract_cols(grad_up_b, back_up)
    grad_mid_part, grad_ffn_gain = norm_back(grad_normed_mid, residual_mid, gain_ffn)
    grad_mid = upstream + grad_mid_part
    grad_attn_raw, grad_post_attn = norm_back(grad_mid, attn_raw, gain_post_attn)
    grad_attn_b = grad_attn_raw.astype(jnp.bfloat16)
    grad_out = contract_rows(own_heads, grad_attn_b)
    heads_grad_b = (
        contract_cols(grad_attn_b, back_out).astype(jnp.bfloat16).reshape(rows, HEADS, HD)
    )
    head_grads = lax.all_to_all(
        jnp.transpose(heads_grad_b, (1, 0, 2)), "head", split_axis=0, concat_axis=0, tiled=True
    )
    delta = jnp.sum(head_grads.astype(jnp.float32) * attended.astype(jnp.float32), axis=-1)

    def score_parts(tile_data, offset):
        scores, allowed = masked_scores(head_queries, tile_data[:, :, :HD], positions, offset)
        probs = jnp.exp(scores - log_norm[..., None])
        prob_grad = jnp.einsum(
            "gid,gjd->gij", head_grads, tile_data[:, :, HD:], preferred_element_type=jnp.float32
        )
        score_grad = (probs * (prob_grad - delta[..., None])).astype(jnp.bfloat16)
        return (probs, score_grad)

    def query_tile(query_sum, tile_data, offset):
        probs, score_grad = score_parts(tile_data, offset)
        return (
            query_sum
            + jnp.einsum(
                "gij,gjd->gid", score_grad, tile_data[:, :, :HD], preferred_element_type=jnp.float32
            )
            * score_scale
        )

    grad_queries = sweep_tiles(
        query_tile, jnp.zeros((seq_count, rows, HD), jnp.float32), all_keyvals, last_pos
    )
    all_logs, all_deltas = (
        lax.all_gather(log_norm, "shard", axis=1, tiled=True),
        lax.all_gather(delta, "shard", axis=1, tiled=True),
    )
    own_keys = head_keyvals[:, :, :HD]
    own_values = head_keyvals[:, :, HD:]
    query_piece = lax.all_gather(head_queries, "shard", axis=1, tiled=True)
    grad_piece = lax.all_gather(head_grads, "shard", axis=1, tiled=True)
    count = query_piece.shape[1]
    tile = math.gcd(count, 2048)
    number = count // tile

    def later_step_tile(index, current):
        offset = index * tile
        query_tile_data = lax.dynamic_slice_in_dim(query_piece, index * tile, tile, 1)
        grad_tile_data = lax.dynamic_slice_in_dim(grad_piece, index * tile, tile, 1)

        def compute(held):
            query_pos = offset + jnp.arange(tile, dtype=jnp.int32)
            logs = lax.dynamic_slice_in_dim(all_logs, offset, tile, 1)
            deltas = lax.dynamic_slice_in_dim(all_deltas, offset, tile, 1)
            scores, allowed = masked_scores(query_tile_data, own_keys, query_pos, first_pos)
            probs = jnp.exp(scores - logs[..., None])
            prob_grad = jnp.einsum(
                "gid,gjd->gij", grad_tile_data, own_values, preferred_element_type=jnp.float32
            )
            score_grad = (probs * (prob_grad - deltas[..., None])).astype(jnp.bfloat16)
            key_part = (
                jnp.einsum(
                    "gij,gid->gjd", score_grad, query_tile_data, preferred_element_type=jnp.float32
                )
                * score_scale
            )
            value_part = jnp.einsum(
                "gij,gid->gjd",
                probs.astype(jnp.bfloat16),
                grad_tile_data,
                preferred_element_type=jnp.float32,
            )
            return held + jnp.concatenate([key_part, value_part], axis=-1)

        return lax.cond(offset + tile - 1 >= first_pos, compute, lambda held: held, current)

    key_grads = lax.fori_loop(
        0, number, later_step_tile, jnp.zeros((seq_count, rows, 2 * HD), jnp.float32)
    )
    query_back, keyval_back = (
        lax.all_to_all(
            grad_queries.astype(jnp.bfloat16), "head", split_axis=0, concat_axis=0, tiled=True
        ).astype(grad_queries.dtype),
        lax.all_to_all(
            key_grads.astype(jnp.bfloat16), "head", split_axis=0, concat_axis=0, tiled=True
        ).astype(key_grads.dtype),
    )
    query_back = jnp.transpose(query_back, (1, 0, 2))
    keyval_sum = jnp.sum(keyval_back, axis=0)
    grad_query_raw, grad_query_gain = norm_back(
        rotate(query_back, positions[:, None], -1.0), query_raw, gain_query
    )
    grad_key_raw, grad_key_gain = norm_back(
        rotate(keyval_sum[:, :HD], positions, -1.0), key_raw, gain_key
    )
    grad_query_b = grad_query_raw.reshape(rows, HEADS * HD).astype(jnp.bfloat16)
    grad_keyval_b = jnp.concatenate([grad_key_raw, keyval_sum[:, HD:]], axis=-1).astype(
        jnp.bfloat16
    )
    grad_query_w = contract_rows(normed_in, grad_query_b)
    grad_keyval_w = contract_rows(normed_in, grad_keyval_b)
    grad_normed_in = contract_cols(grad_query_b, back_query) + contract_cols(
        grad_keyval_b, back_keyval
    )
    grad_in_part, grad_attn_gain = norm_back(grad_normed_in, residual_in, gain_attn)
    grad_input = grad_mid + grad_in_part
    summed = (
        lax.psum_scatter(grad_attn_gain, "shard", scatter_dimension=0, tiled=True),
        lax.psum_scatter(grad_query_gain, "shard", scatter_dimension=0, tiled=True),
        lax.psum_scatter(grad_key_gain, "shard", scatter_dimension=0, tiled=True),
        lax.psum_scatter(grad_post_attn, "shard", scatter_dimension=0, tiled=True),
        lax.psum_scatter(grad_ffn_gain, "shard", scatter_dimension=0, tiled=True),
        lax.psum_scatter(grad_post_ffn, "shard", scatter_dimension=0, tiled=True),
        lax.psum_scatter(grad_query_w, "shard", scatter_dimension=1, tiled=True),
        lax.psum_scatter(grad_keyval_w, "shard", scatter_dimension=1, tiled=True),
        lax.psum_scatter(grad_out, "shard", scatter_dimension=0, tiled=True),
        lax.psum_scatter(grad_gate, "shard", scatter_dimension=1, tiled=True),
        lax.psum_scatter(grad_up, "shard", scatter_dimension=1, tiled=True),
        lax.psum_scatter(grad_down, "shard", scatter_dimension=0, tiled=True),
    )
    summed = (
        lax.psum(summed[0].astype(jnp.bfloat16), "head").astype(jnp.float32),
        lax.psum(summed[1].astype(jnp.bfloat16), "head").astype(jnp.float32),
        lax.psum(summed[2].astype(jnp.bfloat16), "head").astype(jnp.float32),
        lax.psum(summed[3].astype(jnp.bfloat16), "head").astype(jnp.float32),
        lax.psum(summed[4].astype(jnp.bfloat16), "head").astype(jnp.float32),
        lax.psum(summed[5].astype(jnp.bfloat16), "head").astype(jnp.float32),
        lax.psum(summed[6].astype(jnp.bfloat16), "head").astype(jnp.float32),
        lax.psum(summed[7].astype(jnp.bfloat16), "head").astype(jnp.float32),
        lax.psum(summed[8].astype(jnp.bfloat16), "head").astype(jnp.float32),
        lax.psum(summed[9].astype(jnp.bfloat16), "head").astype(jnp.float32),
        lax.psum(summed[10].astype(jnp.bfloat16), "head").astype(jnp.float32),
        lax.psum(summed[11].astype(jnp.bfloat16), "head").astype(jnp.float32),
    )
    return (
        result[None],
        grad_input[None],
        summed[0],
        summed[1],
        summed[2],
        summed[3],
        summed[4],
        summed[5],
        summed[6],
        summed[7],
        summed[8],
        summed[9],
        summed[10],
        summed[11],
    )


BF = jnp.bfloat16
F32 = jnp.float32
VMEM_BYTES = 60 * 1024 * 1024


def dot_nn(left, right):
    return lax.dot_general(
        left, right, (((1,), (0,)), ((), ())), preferred_element_type=jnp.float32
    )


def rms_inv(values):
    return lax.rsqrt(jnp.mean(values * values, axis=-1, keepdims=True) + norm_eps)


def norm_back_rows(upstream, values, gain):
    scale = rms_inv(values)
    weighted = upstream * gain
    inner = jnp.mean(weighted * values, axis=-1, keepdims=True)
    grad_values = scale * weighted - values * (scale * scale * scale) * inner
    grad_gain = jnp.sum(upstream * values * scale, axis=0, keepdims=True)
    return grad_values, grad_gain


def spin(values, cosine, sine):
    half = values.shape[-1] // 2
    first = values[:, :half]
    second = values[:, half:]
    return jnp.concatenate(
        [first * cosine - second * sine, second * cosine + first * sine], axis=-1
    )


def run_block(kernel, outs, ids, *args, scratch=()):
    return pl.pallas_call(
        kernel,
        out_shape=[jax.ShapeDtypeStruct(shape, kind) for shape, kind in outs],
        in_specs=[pl.BlockSpec(memory_space=pltpu.SMEM)]
        + [pl.BlockSpec(memory_space=pltpu.VMEM)] * len(args),
        out_specs=[pl.BlockSpec(memory_space=pltpu.VMEM)] * len(outs),
        scratch_shapes=list(scratch),
        compiler_params=pltpu.CompilerParams(vmem_limit_bytes=VMEM_BYTES),
    )(ids, *args)


def aligned(start, step):
    return pl.multiple_of(start * step, step)


def make_fast(mesh, tokens_shape, widths):
    cols = mesh.shape["head"]
    shards = mesh.shape["shard"]
    chips = shards // 2
    length, dim = tokens_shape[1], tokens_shape[2]
    q_all, kv_all, ff_all = widths
    hd = kv_all // 2
    heads = q_all // hd
    rows = length // shards
    q_own, kv_own, ff_own = q_all // shards, kv_all // shards, ff_all // shards
    q_cut, kv_cut, ff_cut = q_own // cols, kv_own // cols, ff_own // cols
    ff_local = ff_cut * shards
    qkv_cut = q_cut + kv_cut
    qo_cut = 2 * q_cut
    gain_cuts = (dim // shards, hd // shards, hd // shards) + (dim // shards,) * 3

    def swap(x):
        return lax.ppermute(x, "shard", [(s, s ^ 1) for s in range(shards)])

    def along(x, k):
        return lax.ppermute(x, "shard", [(s, s ^ (2 * k)) for s in range(shards)])

    def across(x, m):
        return lax.ppermute(x, "head", [(h, h ^ m) for h in range(cols)])

    def shard_of(ids, r, k):
        return (ids[1] ^ k) * 2 + (ids[2] ^ r)

    def attend_kernel(ids, *refs):
        toks = refs[: 2 * chips]
        packs = refs[2 * chips : 2 * chips + 2 * cols]
        gain_attn, gain_q, gain_k, cos_ref, sin_ref = refs[2 * chips + 2 * cols :][:5]
        (xn_out, wq, wkv, q_out, k_all, v_all, q_raw_out, k_raw_out, p_out, att_out) = refs[
            2 * chips + 2 * cols + 5 :
        ][:10]
        xn_all = refs[-1]
        me = shard_of(ids, 0, 0)
        for r in range(2):
            for m in range(cols):
                pack = packs[r * cols + m]
                for k in range(chips):
                    base = shard_of(ids, r, k) * cols + (ids[0] ^ m)
                    wq[pl.ds(aligned(base, q_cut), q_cut), :] = pack[
                        k * qkv_cut : k * qkv_cut + q_cut, :
                    ]
                    wkv[pl.ds(aligned(base, kv_cut), kv_cut), :] = pack[
                        k * qkv_cut + q_cut : (k + 1) * qkv_cut, :
                    ]
        for r in range(2):
            for k in range(chips):
                tok = toks[r * chips + k][...].astype(F32)
                normed = (tok * rms_inv(tok) * gain_attn[...]).astype(BF)
                xn_all[pl.ds(aligned(shard_of(ids, r, k), rows), rows), :] = normed
                if r == 0 and k == 0:
                    xn_out[...] = normed

        def keys_chunk(i, carry):
            at = pl.ds(aligned(i, 2 * rows), 2 * rows)
            kv = contract_cols(xn_all[at, :], wkv[...])
            key = kv[:, :hd]
            key = key * rms_inv(key) * gain_k[...]
            k_all[at, :] = spin(key, cos_ref[at, :], sin_ref[at, :]).astype(BF)
            v_all[at, :] = kv[:, hd:].astype(BF)
            return carry

        lax.fori_loop(0, chips, keys_chunk, 0)
        own = pl.ds(aligned(me, rows), rows)
        x_own = xn_out[...]
        k_raw_out[...] = contract_cols(x_own, wkv[:hd, :])
        q_raw_out[...] = contract_cols(x_own, wq[...])
        cosine, sine = cos_ref[own, :], sin_ref[own, :]
        query_pos = me * rows + lax.broadcasted_iota(jnp.int32, (rows, length), 0)
        allowed = query_pos >= lax.broadcasted_iota(jnp.int32, (rows, length), 1)
        for n in range(heads):
            raw = q_raw_out[:, n * hd : (n + 1) * hd]
            query = spin(raw * rms_inv(raw) * gain_q[...], cosine, sine).astype(BF)
            q_out[n * rows : (n + 1) * rows, :] = query
            scores = contract_cols(query, k_all[...]) * score_scale
            scores = jnp.where(allowed, scores, -1e30)
            expo = jnp.exp(scores - jnp.max(scores, axis=-1, keepdims=True))
            probs = (expo / jnp.sum(expo, axis=-1, keepdims=True)).astype(BF)
            p_out[n * rows : (n + 1) * rows, :] = probs
            att_out[:, n * hd : (n + 1) * hd] = dot_nn(probs, v_all[...]).astype(BF)

    def out_kernel(ids, att, tok, gain_pa, gain_f, *refs):
        packs = refs[: 2 * cols]
        wo, raw_out, mid_out, xm_out = refs[2 * cols :]
        for r in range(2):
            for m in range(cols):
                for k in range(chips):
                    base = shard_of(ids, r, k) * cols + (ids[0] ^ m)
                    wo[pl.ds(aligned(base, q_cut), q_cut), :] = packs[r * cols + m][
                        k * q_cut : (k + 1) * q_cut, :
                    ]
        raw = dot_nn(att[...], wo[...])
        raw_out[...] = raw
        mid = tok[...].astype(F32) + raw * rms_inv(raw) * gain_pa[...]
        mid_out[...] = mid
        xm_out[...] = (mid * rms_inv(mid) * gain_f[...]).astype(BF)

    def ffn_kernel(ids, *refs):
        xs = refs[:cols]
        packs = refs[cols : cols + shards]
        outs = refs[cols + shards :]
        wg, wu, wd, hid, mul_g, mul_u = outs[:6]
        parts = outs[6:]
        for j in range(shards):
            to = slice(j * ff_cut, (j + 1) * ff_cut)
            wg[to, :] = packs[j][:ff_cut, :]
            wu[to, :] = packs[j][ff_cut : 2 * ff_cut, :]
            wd[to, :] = packs[j][2 * ff_cut :, :]
        for m in range(cols):
            at = slice(m * rows, (m + 1) * rows)
            gate = contract_cols(xs[m][...], wg[...])
            up = contract_cols(xs[m][...], wu[...])
            value, slope = gelu_parts(gate)
            hidden = (value * up).astype(BF)
            parts[m][...] = dot_nn(hidden, wd[...]).astype(parts[m].dtype)
            hid[at, :] = hidden
            mul_g[at, :] = up * slope
            mul_u[at, :] = value

    def head_out_kernel(ids, *refs):
        parts = refs[:cols]
        mid, cot, gain_pf, out, gf_out, gpf_out = refs[cols:]
        raw = parts[0][...]
        for m in range(1, cols):
            raw = raw + parts[m][...].astype(F32)
        out[...] = mid[...] + raw * rms_inv(raw) * gain_pf[...]
        grad, grad_gain = norm_back_rows(cot[...], raw, gain_pf[...])
        gf_out[...] = grad.astype(BF)
        gpf_out[...] = grad_gain

    def ffn_back_kernel(ids, *refs):
        gfs = refs[:cols]
        wg, wu, wd, mul_g, mul_u = refs[cols : cols + 5]
        dg, du = refs[cols + 5 : cols + 7]
        parts = refs[cols + 7 :]
        for m in range(cols):
            at = slice(m * rows, (m + 1) * rows)
            back = contract_cols(gfs[m][...], wd[...])
            grad_g = (back * mul_g[at, :]).astype(BF)
            grad_u = (back * mul_u[at, :]).astype(BF)
            dg[at, :] = grad_g
            du[at, :] = grad_u
            part = dot_nn(grad_g, wg[...]) + dot_nn(grad_u, wu[...])
            parts[m][...] = part.astype(parts[m].dtype)

    def ffn_grads_kernel(ids, *refs):
        xs = refs[:cols]
        gfs = refs[cols : 2 * cols]
        hid, dg, du = refs[2 * cols : 2 * cols + 3]
        keep, send = refs[2 * cols + 3 : 2 * cols + 5]
        stack = refs[2 * cols + 5]
        for part, left, right in ((0, dg, xs), (1, du, xs), (2, hid, gfs)):
            for m in range(cols):
                stack[m * rows : (m + 1) * rows, :] = right[m][...]
            grad = contract_rows(left[...], stack[...])
            for k in range(chips):
                keep[k, part * ff_cut : (part + 1) * ff_cut, :] = grad[
                    k * ff_cut : (k + 1) * ff_cut, :
                ].astype(keep.dtype)
                send[k, part * ff_cut : (part + 1) * ff_cut, :] = grad[
                    (chips + k) * ff_cut : (chips + k + 1) * ff_cut, :
                ].astype(send.dtype)

    def attend_back_kernel(ids, *refs):
        parts = refs[:cols]
        (mid, cot, attn_raw, gain_f, gain_pa, gain_q, wo, att, probs, q_rot, q_raw, k_all) = refs[
            cols : cols + 12
        ]
        v_all, cos_ref, sin_ref = refs[cols + 12 : cols + 15]
        (gmid_out, gab_out, qgb_out, keep, send, gf_gain, gpa_gain, gq_gain) = refs[
            cols + 15 : cols + 23
        ]
        dot_b, ds, dkv = refs[cols + 23 :]
        me = shard_of(ids, 0, 0)
        own = pl.ds(aligned(me, rows), rows)
        total = parts[0][...]
        for m in range(1, cols):
            total = total + parts[m][...].astype(F32)
        grad, gain_grad = norm_back_rows(total, mid[...], gain_f[...])
        gf_gain[...] = gain_grad
        gmid = cot[...] + grad
        gmid_out[...] = gmid
        grad, gain_grad = norm_back_rows(gmid, attn_raw[...], gain_pa[...])
        gpa_gain[...] = gain_grad
        gab = grad.astype(BF)
        gab_out[...] = gab
        cosine, sine = cos_ref[own, :], sin_ref[own, :]
        gq_total = jnp.zeros((1, hd), F32)
        for n in range(heads):
            lanes = slice(n * hd, (n + 1) * hd)
            at = slice(n * rows, (n + 1) * rows)
            d_out = contract_cols(gab, wo[lanes, :]).astype(BF)
            dot_b[at, :] = d_out
            delta = jnp.sum(
                d_out.astype(F32) * att[:, lanes].astype(F32), axis=-1, keepdims=True
            )
            prob_grad = contract_cols(d_out, v_all[...])
            score_grad = (probs[at, :].astype(F32) * (prob_grad - delta)).astype(BF)
            ds[at, :] = score_grad
            q_grad = dot_nn(score_grad, k_all[...]) * score_scale
            q_grad, gain_grad = norm_back_rows(
                spin(q_grad, cosine, -sine), q_raw[:, lanes], gain_q[...]
            )
            gq_total = gq_total + gain_grad
            qgb_out[:, lanes] = q_grad.astype(BF)
        gq_gain[...] = gq_total
        dkv[:, :hd] = contract_rows(ds[...], q_rot[...]) * score_scale
        dkv[:, hd:] = contract_rows(probs[...], dot_b[...])
        for k in range(chips):
            at = pl.ds(aligned(shard_of(ids, 0, k), rows), rows)
            keep[k] = dkv[at, :]
            at = pl.ds(aligned(shard_of(ids, 1, k), rows), rows)
            send[k] = dkv[at, :].astype(BF)

    def pair_kernel(ids, keep, got, *outs):
        for k in range(chips):
            outs[k][...] = (keep[k].astype(F32) + got[k].astype(F32)).astype(outs[k].dtype)

    def proj_grads_kernel(ids, qgb, xn, att, gab, wq, dx, keep, send, gq, go):
        dx[...] = dot_nn(qgb[...], wq[...])
        gq[...] = contract_rows(qgb[...], xn[...])
        go[...] = contract_rows(att[...], gab[...])
        for r, dest in ((0, keep), (1, send)):
            for m in range(cols):
                for k in range(chips):
                    base = shard_of(ids, r, k) * cols + (ids[0] ^ m)
                    at = pl.ds(aligned(base, q_cut), q_cut)
                    dest[m, k * qo_cut : k * qo_cut + q_cut, :] = gq[at, :].astype(dest.dtype)
                    dest[m, k * qo_cut + q_cut : (k + 1) * qo_cut, :] = go[at, :].astype(
                        dest.dtype
                    )

    def split_kernel(ids, keep, got, *outs):
        for m in range(cols):
            outs[m][...] = (keep[m].astype(F32) + got[m].astype(F32)).astype(outs[m].dtype)

    def sum_kernel(count, ids, *refs):
        total = refs[0][...].astype(F32)
        for i in range(1, cols):
            total = total + refs[i][...].astype(F32)
        outs = refs[cols:]
        for k in range(chips):
            outs[k][...] = total[k * count : (k + 1) * count, :].astype(outs[k].dtype)

    def chip_sum_kernel(ids, *refs):
        total = refs[0][...].astype(F32)
        for k in range(1, chips):
            total = total + refs[k][...].astype(F32)
        refs[chips][...] = total.astype(BF)

    def key_back_kernel(ids, *refs):
        parts = refs[:chips]
        (k_raw, gain_k, wkv, dxq, tok, gain_attn, gmid, xn, cos_ref, sin_ref) = refs[
            chips : chips + 10
        ]
        keep, send, gin_out, ga_gain, gk_gain = refs[chips + 10 : chips + 15]
        gkv = refs[chips + 15]
        me = shard_of(ids, 0, 0)
        own = pl.ds(aligned(me, rows), rows)
        total = parts[0][...]
        for k in range(1, chips):
            total = total + parts[k][...].astype(F32)
        grad, gain_grad = norm_back_rows(
            spin(total[:, :hd], cos_ref[own, :], -sin_ref[own, :]), k_raw[...], gain_k[...]
        )
        gk_gain[...] = gain_grad
        kvb = jnp.concatenate([grad, total[:, hd:]], axis=-1).astype(BF)
        gkv[...] = contract_rows(kvb, xn[...])
        for r, dest in ((0, keep), (1, send)):
            for m in range(cols):
                for k in range(chips):
                    base = shard_of(ids, r, k) * cols + (ids[0] ^ m)
                    at = pl.ds(aligned(base, kv_cut), kv_cut)
                    dest[m, k * kv_cut : (k + 1) * kv_cut, :] = gkv[at, :].astype(dest.dtype)
        dx = dxq[...] + dot_nn(kvb, wkv[...])
        grad, gain_grad = norm_back_rows(dx, tok[...].astype(F32), gain_attn[...])
        ga_gain[...] = gain_grad
        gin_out[...] = gmid[...] + grad

    def place_kernel(spec, ids, *refs):
        pieces = refs[:cols]
        outs = refs[cols : cols + len(spec)]
        holds = refs[cols + len(spec) :]
        start = 0
        for (cut, turned), out, hold in zip(spec, outs, holds):
            for m in range(cols):
                hold[pl.ds(aligned(ids[0] ^ m, cut), cut), :] = pieces[m][
                    start : start + cut, :
                ].astype(F32)
            out[...] = hold[...].T if turned else hold[...]
            start += cut

    def place(ids, pieces, spec):
        outs = [
            ((dim, cut * cols) if turned else (cut * cols, dim), F32) for cut, turned in spec
        ]
        scratch = [pltpu.VMEM((cut * cols, dim), F32) for cut, _ in spec]
        return run_block(functools.partial(place_kernel, spec), outs, ids, *pieces, scratch=scratch)

    def reduce_pieces(ids, keep, send, cut):
        got = swap(send)
        shape = (chips * cut, dim)
        outs = [(shape, F32)] + [(shape, BF)] * (cols - 1)
        mine = run_block(split_kernel, outs, ids, keep, got)
        parts = [mine[0]] + [across(mine[m], m) for m in range(1, cols)]
        outs = [((cut, dim), F32)] + [((cut, dim), BF)] * (chips - 1)
        mine = run_block(functools.partial(sum_kernel, cut), outs, ids, *parts)
        parts = [mine[0]] + [along(mine[k], k) for k in range(1, chips)]
        (mine,) = run_block(chip_sum_kernel, [((cut, dim), BF)], ids, *parts)
        return [mine] + [across(mine, m) for m in range(1, cols)]

    def both(x, y):
        return lax.optimization_barrier((x, y))

    def fast_body(
        tokens,
        attn_norm,
        query_norm,
        key_norm,
        post_attn_norm,
        ffn_norm,
        post_ffn_norm,
        query_weight,
        keyval_weight,
        out_weight,
        gate_weight,
        up_weight,
        down_weight,
        cotangent,
    ):
        me_h = lax.axis_index("head").astype(jnp.int32)
        me_s = lax.axis_index("shard").astype(jnp.int32)
        ids = jnp.stack([me_h, me_s // 2, me_s % 2])
        tok, cot = tokens[0], cotangent[0]

        def cut_cols(w, cut):
            return lax.dynamic_slice_in_dim(w, me_h * cut, cut, 1).T

        def cut_rows(w, cut):
            return lax.dynamic_slice_in_dim(w, me_h * cut, cut, 0)

        pack_qkv = jnp.concatenate(
            [cut_cols(query_weight, q_cut), cut_cols(keyval_weight, kv_cut)], axis=0
        )
        pack_out = cut_rows(out_weight, q_cut)
        pack_ffn = jnp.concatenate(
            [
                cut_cols(gate_weight, ff_cut),
                cut_cols(up_weight, ff_cut),
                cut_rows(down_weight, ff_cut),
            ],
            axis=0,
        )
        gains_own = jnp.concatenate(
            [attn_norm, query_norm, key_norm, post_attn_norm, ffn_norm, post_ffn_norm]
        ).reshape(1, -1)

        gain_rows = [gains_own] + [along(gains_own, k) for k in range(1, chips)]
        gain_rows = jnp.concatenate(gain_rows, axis=0)
        gain_rows = jnp.concatenate([gain_rows, swap(gain_rows)], axis=0)
        true_shard = jnp.stack([(ids[1] ^ k) * 2 + (ids[2] ^ r) for r in range(2) for k in range(chips)])
        pick = (jnp.arange(shards, dtype=jnp.int32)[:, None] == true_shard[None, :]).astype(BF)
        gain_rows = jnp.dot(pick, gain_rows, preferred_element_type=F32)
        gains = []
        start = 0
        for cut in gain_cuts:
            gains.append(gain_rows[:, start : start + cut].reshape(1, -1))
            start += cut
        gain_attn, gain_q, gain_k, gain_pa, gain_f, gain_pf = gains

        qkv_z = [pack_qkv] + [along(pack_qkv, k) for k in range(1, chips)]
        tok_z = [tok] + [along(tok, k) for k in range(1, chips)]
        qkv_z = jnp.concatenate(qkv_z, axis=0)
        qkv_h = [qkv_z] + [across(qkv_z, m) for m in range(1, cols)]
        qkv_h = qkv_h + [swap(x) for x in qkv_h]
        toks = tok_z + [swap(x) for x in tok_z]
        pack_out, _ = both(pack_out, qkv_z)
        out_z = [pack_out] + [along(pack_out, k) for k in range(1, chips)]
        out_z = jnp.concatenate(out_z, axis=0)
        out_h = [out_z] + [across(out_z, m) for m in range(1, cols)]
        out_h = out_h + [swap(x) for x in out_h]
        pack_ffn, _ = both(pack_ffn, tok_z[-1])
        ffn_z = [pack_ffn] + [along(pack_ffn, k) for k in range(1, chips)]
        ffn_packs = ffn_z + [swap(x) for x in ffn_z]

        half = hd // 2
        freqs = jnp.exp(
            jnp.arange(half, dtype=F32) * (-2.0 * math.log(rope_base) / hd)
        )
        angles = jnp.arange(length, dtype=jnp.int32).astype(F32)[:, None] * freqs
        cos_all, sin_all = jnp.cos(angles), jnp.sin(angles)

        xn, wq, wkv, q_rot, k_all, v_all, q_raw, k_raw, probs, att = run_block(
            attend_kernel,
            [
                ((rows, dim), BF),
                ((q_all, dim), BF),
                ((kv_all, dim), BF),
                ((heads * rows, hd), BF),
                ((length, hd), BF),
                ((length, hd), BF),
                ((rows, q_all), F32),
                ((rows, hd), F32),
                ((heads * rows, length), BF),
                ((rows, q_all), BF),
            ],
            ids,
            *toks,
            *qkv_h,
            gain_attn,
            gain_q,
            gain_k,
            cos_all,
            sin_all,
            scratch=[pltpu.VMEM((length, dim), BF)],
        )
        wo, attn_raw, mid, xm = run_block(
            out_kernel,
            [((q_all, dim), BF), ((rows, dim), F32), ((rows, dim), F32), ((rows, dim), BF)],
            ids,
            att,
            tok,
            gain_pa,
            gain_f,
            *out_h,
        )
        xs = [xm] + [across(xm, m) for m in range(1, cols)]
        ff_w = ((ff_local, dim), BF)
        part_outs = [((rows, dim), F32)] + [((rows, dim), BF)] * (cols - 1)
        wg, wu, wd, hid, mul_g, mul_u, *parts = run_block(
            ffn_kernel,
            [ff_w, ff_w, ff_w, ((cols * rows, ff_local), BF)]
            + [((cols * rows, ff_local), F32)] * 2
            + part_outs,
            ids,
            *xs,
            *ffn_packs,
        )
        parts = [parts[0]] + [across(parts[m], m) for m in range(1, cols)]
        out, gf, g_pf = run_block(
            head_out_kernel,
            [((rows, dim), F32), ((rows, dim), BF), ((1, dim), F32)],
            ids,
            *parts,
            mid,
            cot,
            gain_pf,
        )
        gfs = [gf] + [across(gf, m) for m in range(1, cols)]
        dg, du, *parts = run_block(
            ffn_back_kernel,
            [((cols * rows, ff_local), BF)] * 2 + part_outs,
            ids,
            *gfs,
            wg,
            wu,
            wd,
            mul_g,
            mul_u,
        )
        parts = [parts[0]] + [across(parts[m], m) for m in range(1, cols)]
        keep, send = run_block(
            ffn_grads_kernel,
            [((chips, 3 * ff_cut, dim), F32), ((chips, 3 * ff_cut, dim), BF)],
            ids,
            *xs,
            *gfs,
            hid,
            dg,
            du,
            scratch=[pltpu.VMEM((cols * rows, dim), BF)],
        )
        got = swap(send)
        ff_piece = (3 * ff_cut, dim)
        mine = run_block(
            pair_kernel, [(ff_piece, F32)] + [(ff_piece, BF)] * (chips - 1), ids, keep, got
        )
        ff_parts = [mine[0]] + [along(mine[k], k) for k in range(1, chips)]
        (ff_sum,) = run_block(chip_sum_kernel, [(ff_piece, BF)], ids, *ff_parts)
        ff_pieces = [ff_sum] + [across(ff_sum, m) for m in range(1, cols)]
        grad_gate, grad_up, grad_down = place(
            ids, ff_pieces, ((ff_cut, True), (ff_cut, True), (ff_cut, False))
        )

        gmid, gab, qgb, keep, send, g_f, g_pa, g_q = run_block(
            attend_back_kernel,
            [
                ((rows, dim), F32),
                ((rows, dim), BF),
                ((rows, q_all), BF),
                ((chips, rows, kv_all), F32),
                ((chips, rows, kv_all), BF),
                ((1, dim), F32),
                ((1, dim), F32),
                ((1, hd), F32),
            ],
            ids,
            *parts,
            mid,
            cot,
            attn_raw,
            gain_f,
            gain_pa,
            gain_q,
            wo,
            att,
            probs,
            q_rot,
            q_raw,
            k_all,
            v_all,
            cos_all,
            sin_all,
            scratch=[
                pltpu.VMEM((heads * rows, hd), BF),
                pltpu.VMEM((heads * rows, length), BF),
                pltpu.VMEM((length, kv_all), F32),
            ],
        )
        got = swap(send)
        kv_piece = (rows, kv_all)
        mine = run_block(
            pair_kernel, [(kv_piece, F32)] + [(kv_piece, BF)] * (chips - 1), ids, keep, got
        )
        kv_parts = [mine[0]] + [along(mine[k], k) for k in range(1, chips)]
        dxq, keep, send = run_block(
            proj_grads_kernel,
            [
                ((rows, dim), F32),
                ((cols, chips * qo_cut, dim), BF),
                ((cols, chips * qo_cut, dim), BF),
            ],
            ids,
            qgb,
            xn,
            att,
            gab,
            wq,
            scratch=[pltpu.VMEM((q_all, dim), F32), pltpu.VMEM((q_all, dim), F32)],
        )
        qo_pieces = reduce_pieces(ids, keep, send, qo_cut)
        grad_query_w, grad_out = place(ids, qo_pieces, ((q_cut, True), (q_cut, False)))
        keep, send, grad_input, g_a, g_k = run_block(
            key_back_kernel,
            [
                ((cols, chips * kv_cut, dim), BF),
                ((cols, chips * kv_cut, dim), BF),
                ((rows, dim), F32),
                ((1, dim), F32),
                ((1, hd), F32),
            ],
            ids,
            *kv_parts,
            k_raw,
            gain_k,
            wkv,
            dxq,
            tok,
            gain_attn,
            gmid,
            xn,
            cos_all,
            sin_all,
            scratch=[pltpu.VMEM((kv_all, dim), F32)],
        )
        kv_pieces = reduce_pieces(ids, keep, send, kv_cut)
        (grad_keyval_w,) = place(ids, kv_pieces, ((kv_cut, True),))

        gain_grads = jnp.concatenate(
            [
                g.reshape(shards, cut)
                for g, cut in zip((g_a, g_q, g_k, g_pa, g_f, g_pf), gain_cuts)
            ],
            axis=1,
        )
        gain_grads = gain_grads + swap(gain_grads)
        gain_grads = functools.reduce(
            jnp.add, [gain_grads] + [along(gain_grads, k) for k in range(1, chips)]
        )
        gain_grads = functools.reduce(
            jnp.add, [gain_grads] + [across(gain_grads, m) for m in range(1, cols)]
        )
        gain_own = lax.dynamic_slice_in_dim(gain_grads, me_s, 1, 0)[0]
        small = []
        start = 0
        for cut in gain_cuts:
            small.append(gain_own[start : start + cut])
            start += cut
        return (
            out[None],
            grad_input[None],
            *small,
            grad_query_w,
            grad_keyval_w,
            grad_out,
            grad_gate,
            grad_up,
            grad_down,
        )

    return fast_body


def power_of_two(number):
    return number & (number - 1) == 0


def direct_fits(mesh, tokens, query_weight, keyval_weight, gate_weight):
    cols, shards = mesh.shape["head"], mesh.shape["shard"]
    parts = cols * shards
    return (
        power_of_two(cols)
        and power_of_two(shards)
        and cols <= 4
        and 2 <= shards <= 8
        and tokens.shape[1] <= 1024
        and tokens.shape[2] % 128 == 0
        and tokens.shape[1] % (16 * shards) == 0
        and keyval_weight.shape[1] % 512 == 0
        and all(w.shape[1] % (16 * parts) == 0 for w in (query_weight, keyval_weight, gate_weight))
    )


def solution(mesh):
    placed = (
        P("head", "shard", None),
        P("shard"),
        P("shard"),
        P("shard"),
        P("shard"),
        P("shard"),
        P("shard"),
        P(None, "shard"),
        P(None, "shard"),
        P("shard", None),
        P(None, "shard"),
        P(None, "shard"),
        P("shard", None),
        P("head", "shard", None),
    )
    def run(*args):
        tokens, query_weight, keyval_weight, gate_weight = args[0], args[7], args[8], args[10]
        inner = body
        if direct_fits(mesh, tokens, query_weight, keyval_weight, gate_weight):
            widths = (query_weight.shape[1], keyval_weight.shape[1], gate_weight.shape[1])
            inner = make_fast(mesh, tokens.shape, widths)
        return jax.shard_map(
            inner,
            mesh=mesh,
            in_specs=placed,
            out_specs=(
                P("head", "shard", None),
                P("head", "shard", None),
                P("shard"),
                P("shard"),
                P("shard"),
                P("shard"),
                P("shard"),
                P("shard"),
                P(None, "shard"),
                P(None, "shard"),
                P("shard", None),
                P(None, "shard"),
                P(None, "shard"),
                P("shard", None),
            ),
            check_vma=False,
        )(*args)

    return run
```

```python
import functools
import math

import jax
import jax.numpy as jnp
from jax import lax
from jax.experimental import pallas as pl
from jax.experimental.pallas import tpu as pltpu
from jax.sharding import PartitionSpec as P

HEADS = 4
HD = 256


norm_eps = 1e-06
rope_base = 1000000.0
score_scale = 0.0625
gelu_coef = 0.7978845608028654


def rms_scale(values):
    return lax.rsqrt(jnp.mean(values * values, axis=-1, keepdims=True) + norm_eps)


def norm_back(upstream, values, gain):
    scale = rms_scale(values)
    weighted = upstream * gain
    inner = jnp.mean(weighted * values, axis=-1, keepdims=True)
    grad_values = scale * weighted - values * (scale * scale * scale) * inner
    leading = tuple(range(values.ndim - 1))
    grad_gain = jnp.sum(upstream * values * scale, axis=leading)
    return (grad_values, grad_gain)


def rotate(values, positions, direction):
    half = values.shape[-1] // 2
    index = jnp.arange(half, dtype=jnp.float32)
    freqs = jnp.exp(index * (-2.0 * math.log(rope_base) / values.shape[-1]))
    angles = positions.astype(jnp.float32)[..., None] * freqs
    cosine = jnp.cos(angles)
    sine = direction * jnp.sin(angles)
    first = values[..., :half]
    second = values[..., half:]
    return jnp.concatenate(
        [first * cosine - second * sine, second * cosine + first * sine], axis=-1
    )


def gelu_parts(values):
    inner = gelu_coef * (values + 0.044715 * values * values * values)
    tanh_value = jnp.tanh(inner)
    value = 0.5 * values * (1.0 + tanh_value)
    slope = 0.5 * (1.0 + tanh_value) + 0.5 * values * (
        1.0 - tanh_value * tanh_value
    ) * gelu_coef * (1.0 + 3.0 * 0.044715 * values * values)
    return (value, slope)


def contract_rows(left, right):
    return lax.dot_general(
        left, right, (((0,), (0,)), ((), ())), preferred_element_type=jnp.float32
    )


def contract_cols(left, right):
    return lax.dot_general(
        left, right, (((1,), (1,)), ((), ())), preferred_element_type=jnp.float32
    )


def masked_scores(queries, keys, query_pos, key_start):
    scores = (
        jnp.einsum("gid,gjd->gij", queries, keys, preferred_element_type=jnp.float32) * score_scale
    )
    key_pos = key_start + jnp.arange(keys.shape[1], dtype=jnp.int32)
    allowed = query_pos[:, None] >= key_pos[None, :]
    return (jnp.where(allowed[None], scores, -1e30), allowed)


def sweep_tiles(visit, state, piece, last_pos):
    count = piece.shape[1]
    tile = math.gcd(count, 2048)
    number = count // tile

    def sweep_step_tile(index, current):
        offset = index * tile
        tile_data = lax.dynamic_slice_in_dim(piece, index * tile, tile, 1)
        return lax.cond(
            offset <= last_pos,
            lambda held: visit(held, tile_data, offset),
            lambda held: held,
            current,
        )

    return lax.fori_loop(0, number, sweep_step_tile, state)


def body(
    tokens,
    attn_norm,
    query_norm,
    key_norm,
    post_attn_norm,
    ffn_norm,
    post_ffn_norm,
    query_weight,
    keyval_weight,
    out_weight,
    gate_weight,
    up_weight,
    down_weight,
    cotangent,
):
    gathered = (
        lax.all_gather(attn_norm, "shard", axis=0, tiled=True),
        lax.all_gather(query_norm, "shard", axis=0, tiled=True),
        lax.all_gather(key_norm, "shard", axis=0, tiled=True),
        lax.all_gather(post_attn_norm, "shard", axis=0, tiled=True),
        lax.all_gather(ffn_norm, "shard", axis=0, tiled=True),
        lax.all_gather(post_ffn_norm, "shard", axis=0, tiled=True),
        lax.all_gather(query_weight, "shard", axis=1, tiled=True),
        lax.all_gather(keyval_weight, "shard", axis=1, tiled=True),
        lax.all_gather(out_weight, "shard", axis=0, tiled=True),
        lax.all_gather(gate_weight, "shard", axis=1, tiled=True),
        lax.all_gather(up_weight, "shard", axis=1, tiled=True),
        lax.all_gather(down_weight, "shard", axis=0, tiled=True),
    )
    gain_attn, gain_query, gain_key, gain_post_attn, gain_ffn, gain_post_ffn = [
        g.astype(jnp.float32) for g in gathered[:6]
    ]
    full_query, full_keyval, full_out, full_gate, full_up, full_down = gathered[6:]
    back_query, back_keyval, back_out, back_gate, back_up, back_down = gathered[6:]
    rows = tokens.shape[1]
    positions = lax.axis_index("shard") * rows + jnp.arange(rows, dtype=jnp.int32)
    first_pos = positions[0]
    last_pos = positions[rows - 1]
    residual_in = tokens[0].astype(jnp.float32)
    normed_in = (residual_in * rms_scale(residual_in) * gain_attn).astype(jnp.bfloat16)
    query_raw = jnp.dot(normed_in, full_query, preferred_element_type=jnp.float32).reshape(
        rows, HEADS, HD
    )
    keyval_raw = jnp.dot(normed_in, full_keyval, preferred_element_type=jnp.float32)
    key_raw = keyval_raw[:, :HD]
    query_rot = rotate(
        query_raw * rms_scale(query_raw) * gain_query, positions[:, None], 1.0
    ).astype(jnp.bfloat16)
    key_rot = rotate(key_raw * rms_scale(key_raw) * gain_key, positions, 1.0).astype(jnp.bfloat16)
    keyval_rot = jnp.concatenate([key_rot, keyval_raw[:, HD:].astype(jnp.bfloat16)], axis=-1)
    query_heads_first = jnp.transpose(query_rot, (1, 0, 2))
    keyval_copies = jnp.broadcast_to(keyval_rot[None], (HEADS, rows, 2 * HD))
    head_queries, head_keyvals = (
        lax.all_to_all(query_heads_first, "head", split_axis=0, concat_axis=0, tiled=True),
        lax.all_to_all(keyval_copies, "head", split_axis=0, concat_axis=0, tiled=True),
    )
    seq_count = head_queries.shape[0]

    def online_tile(state, tile_data, offset):
        running_max, running_sum, weighted = state
        scores, allowed = masked_scores(head_queries, tile_data[:, :, :HD], positions, offset)
        new_max = jnp.maximum(running_max, jnp.max(scores, axis=-1))
        probs = jnp.where(allowed[None], jnp.exp(scores - new_max[..., None]), 0.0)
        fade = jnp.exp(running_max - new_max)
        running_sum = running_sum * fade + jnp.sum(probs, axis=-1)
        weighted = weighted * fade[..., None] + jnp.einsum(
            "gij,gjd->gid",
            probs.astype(jnp.bfloat16),
            tile_data[:, :, HD:],
            preferred_element_type=jnp.float32,
        )
        return (new_max, running_sum, weighted)

    start_state = (
        jnp.full((seq_count, rows), -1e30, jnp.float32),
        jnp.zeros((seq_count, rows), jnp.float32),
        jnp.zeros((seq_count, rows, HD), jnp.float32),
    )
    all_keyvals = lax.all_gather(head_keyvals, "shard", axis=1, tiled=True)
    final_state = sweep_tiles(online_tile, start_state, all_keyvals, last_pos)
    top_score, total_weight, weighted_sum = final_state
    attended = (weighted_sum / total_weight[..., None]).astype(jnp.bfloat16)
    log_norm = top_score + jnp.log(total_weight)
    returned = lax.all_to_all(attended, "head", split_axis=0, concat_axis=0, tiled=True)
    own_heads = jnp.transpose(returned, (1, 0, 2)).reshape(rows, HEADS * HD)
    attn_raw = jnp.dot(own_heads, full_out, preferred_element_type=jnp.float32)
    residual_mid = residual_in + attn_raw * rms_scale(attn_raw) * gain_post_attn
    normed_mid = (residual_mid * rms_scale(residual_mid) * gain_ffn).astype(jnp.bfloat16)
    gate_raw = jnp.dot(normed_mid, full_gate, preferred_element_type=jnp.float32)
    up_raw = jnp.dot(normed_mid, full_up, preferred_element_type=jnp.float32)
    gelu_value, gelu_slope = gelu_parts(gate_raw)
    hidden = (gelu_value * up_raw).astype(jnp.bfloat16)
    ffn_raw = jnp.dot(hidden, full_down, preferred_element_type=jnp.float32)
    result = residual_mid + ffn_raw * rms_scale(ffn_raw) * gain_post_ffn
    upstream = cotangent[0]
    grad_ffn_raw, grad_post_ffn = norm_back(upstream, ffn_raw, gain_post_ffn)
    grad_ffn_b = grad_ffn_raw.astype(jnp.bfloat16)
    grad_down = contract_rows(hidden, grad_ffn_b)
    grad_hidden = contract_cols(grad_ffn_b, back_down)
    grad_gate_b = (grad_hidden * up_raw * gelu_slope).astype(jnp.bfloat16)
    grad_up_b = (grad_hidden * gelu_value).astype(jnp.bfloat16)
    grad_gate = contract_rows(normed_mid, grad_gate_b)
    grad_up = contract_rows(normed_mid, grad_up_b)
    grad_normed_mid = contract_cols(grad_gate_b, back_gate) + contract_cols(grad_up_b, back_up)
    grad_mid_part, grad_ffn_gain = norm_back(grad_normed_mid, residual_mid, gain_ffn)
    grad_mid = upstream + grad_mid_part
    grad_attn_raw, grad_post_attn = norm_back(grad_mid, attn_raw, gain_post_attn)
    grad_attn_b = grad_attn_raw.astype(jnp.bfloat16)
    grad_out = contract_rows(own_heads, grad_attn_b)
    heads_grad_b = (
        contract_cols(grad_attn_b, back_out).astype(jnp.bfloat16).reshape(rows, HEADS, HD)
    )
    head_grads = lax.all_to_all(
        jnp.transpose(heads_grad_b, (1, 0, 2)), "head", split_axis=0, concat_axis=0, tiled=True
    )
    delta = jnp.sum(head_grads.astype(jnp.float32) * attended.astype(jnp.float32), axis=-1)

    def score_parts(tile_data, offset):
        scores, _ = masked_scores(head_queries, tile_data[:, :, :HD], positions, offset)
        probs = jnp.exp(scores - log_norm[..., None])
        prob_grad = jnp.einsum(
            "gid,gjd->gij", head_grads, tile_data[:, :, HD:], preferred_element_type=jnp.float32
        )
        score_grad = (probs * (prob_grad - delta[..., None])).astype(jnp.bfloat16)
        return (probs, score_grad)

    def query_tile(query_sum, tile_data, offset):
        _, score_grad = score_parts(tile_data, offset)
        return (
            query_sum
            + jnp.einsum(
                "gij,gjd->gid", score_grad, tile_data[:, :, :HD], preferred_element_type=jnp.float32
            )
            * score_scale
        )

    grad_queries = sweep_tiles(
        query_tile, jnp.zeros((seq_count, rows, HD), jnp.float32), all_keyvals, last_pos
    )
    all_logs, all_deltas = (
        lax.all_gather(log_norm, "shard", axis=1, tiled=True),
        lax.all_gather(delta, "shard", axis=1, tiled=True),
    )
    own_keys = head_keyvals[:, :, :HD]
    own_values = head_keyvals[:, :, HD:]
    query_piece = lax.all_gather(head_queries, "shard", axis=1, tiled=True)
    grad_piece = lax.all_gather(head_grads, "shard", axis=1, tiled=True)
    count = query_piece.shape[1]
    tile = math.gcd(count, 2048)
    number = count // tile

    def later_step_tile(index, current):
        offset = index * tile
        query_tile_data = lax.dynamic_slice_in_dim(query_piece, index * tile, tile, 1)
        grad_tile_data = lax.dynamic_slice_in_dim(grad_piece, index * tile, tile, 1)

        def compute(held):
            query_pos = offset + jnp.arange(tile, dtype=jnp.int32)
            logs = lax.dynamic_slice_in_dim(all_logs, offset, tile, 1)
            deltas = lax.dynamic_slice_in_dim(all_deltas, offset, tile, 1)
            scores, _ = masked_scores(query_tile_data, own_keys, query_pos, first_pos)
            probs = jnp.exp(scores - logs[..., None])
            prob_grad = jnp.einsum(
                "gid,gjd->gij", grad_tile_data, own_values, preferred_element_type=jnp.float32
            )
            score_grad = (probs * (prob_grad - deltas[..., None])).astype(jnp.bfloat16)
            key_part = (
                jnp.einsum(
                    "gij,gid->gjd", score_grad, query_tile_data, preferred_element_type=jnp.float32
                )
                * score_scale
            )
            value_part = jnp.einsum(
                "gij,gid->gjd",
                probs.astype(jnp.bfloat16),
                grad_tile_data,
                preferred_element_type=jnp.float32,
            )
            return held + jnp.concatenate([key_part, value_part], axis=-1)

        return lax.cond(offset + tile - 1 >= first_pos, compute, lambda held: held, current)

    key_grads = lax.fori_loop(
        0, number, later_step_tile, jnp.zeros((seq_count, rows, 2 * HD), jnp.float32)
    )
    query_back, keyval_back = (
        lax.all_to_all(
            grad_queries.astype(jnp.bfloat16), "head", split_axis=0, concat_axis=0, tiled=True
        ).astype(grad_queries.dtype),
        lax.all_to_all(
            key_grads.astype(jnp.bfloat16), "head", split_axis=0, concat_axis=0, tiled=True
        ).astype(key_grads.dtype),
    )
    query_back = jnp.transpose(query_back, (1, 0, 2))
    keyval_sum = jnp.sum(keyval_back, axis=0)
    grad_query_raw, grad_query_gain = norm_back(
        rotate(query_back, positions[:, None], -1.0), query_raw, gain_query
    )
    grad_key_raw, grad_key_gain = norm_back(
        rotate(keyval_sum[:, :HD], positions, -1.0), key_raw, gain_key
    )
    grad_query_b = grad_query_raw.reshape(rows, HEADS * HD).astype(jnp.bfloat16)
    grad_keyval_b = jnp.concatenate([grad_key_raw, keyval_sum[:, HD:]], axis=-1).astype(
        jnp.bfloat16
    )
    grad_query_w = contract_rows(normed_in, grad_query_b)
    grad_keyval_w = contract_rows(normed_in, grad_keyval_b)
    grad_normed_in = contract_cols(grad_query_b, back_query) + contract_cols(
        grad_keyval_b, back_keyval
    )
    grad_in_part, grad_attn_gain = norm_back(grad_normed_in, residual_in, gain_attn)
    grad_input = grad_mid + grad_in_part
    summed = (
        lax.psum_scatter(grad_attn_gain, "shard", scatter_dimension=0, tiled=True),
        lax.psum_scatter(grad_query_gain, "shard", scatter_dimension=0, tiled=True),
        lax.psum_scatter(grad_key_gain, "shard", scatter_dimension=0, tiled=True),
        lax.psum_scatter(grad_post_attn, "shard", scatter_dimension=0, tiled=True),
        lax.psum_scatter(grad_ffn_gain, "shard", scatter_dimension=0, tiled=True),
        lax.psum_scatter(grad_post_ffn, "shard", scatter_dimension=0, tiled=True),
        lax.psum_scatter(grad_query_w, "shard", scatter_dimension=1, tiled=True),
        lax.psum_scatter(grad_keyval_w, "shard", scatter_dimension=1, tiled=True),
        lax.psum_scatter(grad_out, "shard", scatter_dimension=0, tiled=True),
        lax.psum_scatter(grad_gate, "shard", scatter_dimension=1, tiled=True),
        lax.psum_scatter(grad_up, "shard", scatter_dimension=1, tiled=True),
        lax.psum_scatter(grad_down, "shard", scatter_dimension=0, tiled=True),
    )
    summed = (
        lax.psum(summed[0].astype(jnp.bfloat16), "head").astype(jnp.float32),
        lax.psum(summed[1].astype(jnp.bfloat16), "head").astype(jnp.float32),
        lax.psum(summed[2].astype(jnp.bfloat16), "head").astype(jnp.float32),
        lax.psum(summed[3].astype(jnp.bfloat16), "head").astype(jnp.float32),
        lax.psum(summed[4].astype(jnp.bfloat16), "head").astype(jnp.float32),
        lax.psum(summed[5].astype(jnp.bfloat16), "head").astype(jnp.float32),
        lax.psum(summed[6].astype(jnp.bfloat16), "head").astype(jnp.float32),
        lax.psum(summed[7].astype(jnp.bfloat16), "head").astype(jnp.float32),
        lax.psum(summed[8].astype(jnp.bfloat16), "head").astype(jnp.float32),
        lax.psum(summed[9].astype(jnp.bfloat16), "head").astype(jnp.float32),
        lax.psum(summed[10].astype(jnp.bfloat16), "head").astype(jnp.float32),
        lax.psum(summed[11].astype(jnp.bfloat16), "head").astype(jnp.float32),
    )
    return (
        result[None],
        grad_input[None],
        summed[0],
        summed[1],
        summed[2],
        summed[3],
        summed[4],
        summed[5],
        summed[6],
        summed[7],
        summed[8],
        summed[9],
        summed[10],
        summed[11],
    )


BF = jnp.bfloat16
F32 = jnp.float32
MIB = 1024 * 1024


def dot_nn(left, right):
    return lax.dot_general(
        left, right, (((1,), (0,)), ((), ())), preferred_element_type=jnp.float32
    )


def rms_inv(values):
    return lax.rsqrt(jnp.mean(values * values, axis=-1, keepdims=True) + norm_eps)


def norm_back_rows(upstream, values, gain):
    scale = rms_inv(values)
    weighted = upstream * gain
    inner = jnp.mean(weighted * values, axis=-1, keepdims=True)
    grad_values = scale * weighted - values * (scale * scale * scale) * inner
    grad_gain = jnp.sum(upstream * values * scale, axis=0, keepdims=True)
    return grad_values, grad_gain


def spin(values, cosine, sine):
    half = values.shape[-1] // 2
    first = values[:, :half]
    second = values[:, half:]
    return jnp.concatenate(
        [first * cosine - second * sine, second * cosine + first * sine], axis=-1
    )


def padded_bytes(shape, kind):
    size = jnp.dtype(kind).itemsize
    return math.prod(shape[:-2]) * max(shape[-2], 16) * max(shape[-1], 128) * size


def run_block(kernel, outs, ids, *args, scratch=(), slack=4):
    held = sum(padded_bytes(x.shape, x.dtype) for x in args)
    held += sum(padded_bytes(shape, kind) for shape, kind in outs)
    held += sum(padded_bytes(x.shape, x.dtype) for x in scratch)
    return pl.pallas_call(
        kernel,
        out_shape=[jax.ShapeDtypeStruct(shape, kind) for shape, kind in outs],
        in_specs=[pl.BlockSpec(memory_space=pltpu.SMEM)]
        + [pl.BlockSpec(memory_space=pltpu.VMEM)] * len(args),
        out_specs=[pl.BlockSpec(memory_space=pltpu.VMEM)] * len(outs),
        scratch_shapes=list(scratch),
        compiler_params=pltpu.CompilerParams(vmem_limit_bytes=held + slack * MIB),
    )(ids, *args)


def aligned(start, step):
    return pl.multiple_of(start * step, step)


def make_fast(mesh, tokens_shape, widths):
    cols = mesh.shape["head"]
    shards = mesh.shape["shard"]
    chips = shards // 2
    length, dim = tokens_shape[1], tokens_shape[2]
    q_all, kv_all, ff_all = widths
    hd = kv_all // 2
    heads = q_all // hd
    rows = length // shards
    q_own, kv_own, ff_own = q_all // shards, kv_all // shards, ff_all // shards
    q_cut, kv_cut, ff_cut = q_own // cols, kv_own // cols, ff_own // cols
    ff_local = ff_cut * shards
    qkv_cut = q_cut + kv_cut
    gain_cuts = (dim // shards, hd // shards, hd // shards) + (dim // shards,) * 3

    def swap(x):
        return lax.ppermute(x, "shard", [(s, s ^ 1) for s in range(shards)])

    def along(x, k):
        return lax.ppermute(x, "shard", [(s, s ^ (2 * k)) for s in range(shards)])

    def across(x, m):
        return lax.ppermute(x, "head", [(h, h ^ m) for h in range(cols)])

    def all_along(x):
        return [x] + [along(x, k) for k in range(1, chips)]

    def all_across(x):
        return [x] + [across(x, m) for m in range(1, cols)]

    def trade_along(xs):
        return [xs[0]] + [along(xs[k], k) for k in range(1, chips)]

    def trade_across(xs):
        return [xs[0]] + [across(xs[m], m) for m in range(1, cols)]

    def with_partner(xs):
        return list(xs) + [swap(x) for x in xs]

    def shard_of(ids, r, k):
        return (ids[1] ^ k) * 2 + (ids[2] ^ r)

    def pack_qkv_kernel(ids, wq, wkv_t, out, hold_q, hold_kv):
        hold_q[...] = wq[...].astype(F32).T
        hold_kv[...] = wkv_t[...].astype(F32)
        out[:q_cut, :] = hold_q[pl.ds(aligned(ids[0], q_cut), q_cut), :].astype(BF)
        out[q_cut:, :] = hold_kv[pl.ds(aligned(ids[0], kv_cut), kv_cut), :].astype(BF)

    def pack_out_kernel(ids, wo, gains, out):
        out[:q_cut, :] = wo[pl.ds(aligned(ids[0], q_cut), q_cut), :]
        out[q_cut:, :] = jnp.zeros((16, dim), BF)
        rows_of = jnp.concatenate([gains[...], jnp.zeros((8, 128), F32)], axis=0)
        out[q_cut:, :128] = rows_of.astype(BF)

    def pack_ffn_kernel(ids, wg, wu, wd, out, hold):
        at = pl.ds(aligned(ids[0], ff_cut), ff_cut)
        hold[...] = wg[...].astype(F32).T
        out[:ff_cut, :] = hold[at, :].astype(BF)
        hold[...] = wu[...].astype(F32).T
        out[ff_cut : 2 * ff_cut, :] = hold[at, :].astype(BF)
        out[2 * ff_cut :, :] = wd[at, :]

    def stage_out_kernel(ids, *refs):
        out, gain_block = refs[chips:]
        for k in range(chips):
            out[k * q_cut : (k + 1) * q_cut, :] = refs[k][:q_cut, :]
            gain_block[k * 16 : (k + 1) * 16, :] = refs[k][q_cut:, :128]

    def owner_rows(ids, row):
        k, r = row % chips, row // chips
        return (ids[1] ^ k) * 2 + (ids[2] ^ r)

    def gains_kernel(ids, near, far, wide_e, wide_s, thin_e, thin_s, *outs):
        near, far = near[...].astype(F32), far[...].astype(F32)
        lane_rows = lax.broadcasted_iota(jnp.int32, (shards, 1), 0)
        owner = jnp.zeros((shards, 1), jnp.int32)
        for row in range(shards):
            owner = jnp.where(lane_rows == row, owner_rows(ids, row), owner)
        for g, out in enumerate(outs):
            block = jnp.concatenate(
                [
                    part[k * 16 + g : k * 16 + g + 1, :]
                    for part in (near, far)
                    for k in range(chips)
                ],
                axis=0,
            ).astype(BF)
            expand, seg = (wide_e, wide_s) if gain_cuts[g] == gain_cuts[0] else (thin_e, thin_s)
            spread = dot_nn(block, expand[...])
            out[...] = jnp.sum(jnp.where(seg[...] == owner, spread, 0.0), axis=0, keepdims=True)

    def attend_kernel(ids, *refs):
        toks = refs[: 2 * chips]
        packs = refs[2 * chips : 2 * chips + 2 * cols]
        gain_attn, gain_q, gain_k, cos_ref, sin_ref = refs[2 * chips + 2 * cols :][:5]
        (xn_out, wq, wkv, q_out, k_all, v_all, q_raw_out, k_raw_out, p_out, att_out, xn_all) = refs[
            2 * chips + 2 * cols + 5 :
        ]
        me = shard_of(ids, 0, 0)
        for r in range(2):
            for m in range(cols):
                pack = packs[r * cols + m]
                for k in range(chips):
                    base = shard_of(ids, r, k) * cols + (ids[0] ^ m)
                    wq[pl.ds(aligned(base, q_cut), q_cut), :] = pack[
                        k * qkv_cut : k * qkv_cut + q_cut, :
                    ]
                    wkv[pl.ds(aligned(base, kv_cut), kv_cut), :] = pack[
                        k * qkv_cut + q_cut : (k + 1) * qkv_cut, :
                    ]
        for r in range(2):
            for k in range(chips):
                tok = toks[r * chips + k][...].astype(F32)
                normed = (tok * rms_inv(tok) * gain_attn[...]).astype(BF)
                xn_all[pl.ds(aligned(shard_of(ids, r, k), rows), rows), :] = normed
                if r == 0 and k == 0:
                    xn_out[...] = normed

        def keys_chunk(i, carry):
            at = pl.ds(aligned(i, 2 * rows), 2 * rows)
            kv = contract_cols(xn_all[at, :], wkv[...])
            key = kv[:, :hd]
            key = key * rms_inv(key) * gain_k[...]
            k_all[at, :] = spin(key, cos_ref[at, :], sin_ref[at, :]).astype(BF)
            v_all[at, :] = kv[:, hd:].astype(BF)
            return carry

        lax.fori_loop(0, chips, keys_chunk, 0)
        own = pl.ds(aligned(me, rows), rows)
        x_own = xn_out[...]
        k_raw_out[...] = contract_cols(x_own, wkv[:hd, :])
        q_raw_out[...] = contract_cols(x_own, wq[...])
        cosine, sine = cos_ref[own, :], sin_ref[own, :]
        query_pos = me * rows + lax.broadcasted_iota(jnp.int32, (rows, length), 0)
        allowed = query_pos >= lax.broadcasted_iota(jnp.int32, (rows, length), 1)
        for n in range(heads):
            raw = q_raw_out[:, n * hd : (n + 1) * hd]
            query = spin(raw * rms_inv(raw) * gain_q[...], cosine, sine).astype(BF)
            q_out[n * rows : (n + 1) * rows, :] = query
            scores = contract_cols(query, k_all[...]) * score_scale
            scores = jnp.where(allowed, scores, -1e30)
            expo = jnp.exp(scores - jnp.max(scores, axis=-1, keepdims=True))
            probs = (expo / jnp.sum(expo, axis=-1, keepdims=True)).astype(BF)
            p_out[n * rows : (n + 1) * rows, :] = probs
            att_out[:, n * hd : (n + 1) * hd] = dot_nn(probs, v_all[...]).astype(BF)

    def out_kernel(ids, att, tok, gain_pa, gain_f, *refs):
        packs = refs[: 2 * cols]
        wo, raw_out, mid_out, xm_out = refs[2 * cols :]
        for r in range(2):
            for m in range(cols):
                for k in range(chips):
                    base = shard_of(ids, r, k) * cols + (ids[0] ^ m)
                    wo[pl.ds(aligned(base, q_cut), q_cut), :] = packs[r * cols + m][
                        k * q_cut : (k + 1) * q_cut, :
                    ]
        raw = dot_nn(att[...], wo[...])
        raw_out[...] = raw
        mid = tok[...].astype(F32) + raw * rms_inv(raw) * gain_pa[...]
        mid_out[...] = mid
        xm_out[...] = (mid * rms_inv(mid) * gain_f[...]).astype(BF)

    def ffn_kernel(ids, *refs):
        xs = refs[:cols]
        packs = refs[cols : cols + shards]
        outs = refs[cols + shards :]
        wg, wu, wd, hid, mul_g, mul_u = outs[:6]
        parts = outs[6:]
        for j in range(shards):
            to = slice(j * ff_cut, (j + 1) * ff_cut)
            wg[to, :] = packs[j][:ff_cut, :]
            wu[to, :] = packs[j][ff_cut : 2 * ff_cut, :]
            wd[to, :] = packs[j][2 * ff_cut :, :]
        for m in range(cols):
            at = slice(m * rows, (m + 1) * rows)
            gate = contract_cols(xs[m][...], wg[...])
            up = contract_cols(xs[m][...], wu[...])
            value, slope = gelu_parts(gate)
            hidden = (value * up).astype(BF)
            parts[m][...] = dot_nn(hidden, wd[...]).astype(parts[m].dtype)
            hid[at, :] = hidden
            mul_g[at, :] = up * slope
            mul_u[at, :] = value

    def head_out_kernel(ids, *refs):
        parts = refs[:cols]
        mid, cot, gain_pf, out, gf_out, gpf_out = refs[cols:]
        raw = parts[0][...]
        for m in range(1, cols):
            raw = raw + parts[m][...].astype(F32)
        out[...] = mid[...] + raw * rms_inv(raw) * gain_pf[...]
        grad, grad_gain = norm_back_rows(cot[...], raw, gain_pf[...])
        gf_out[...] = grad.astype(BF)
        gpf_out[...] = grad_gain

    def ffn_back_kernel(ids, *refs):
        gfs = refs[:cols]
        wg, wu, wd, mul_g, mul_u = refs[cols : cols + 5]
        dg, du = refs[cols + 5 : cols + 7]
        parts = refs[cols + 7 :]
        for m in range(cols):
            at = slice(m * rows, (m + 1) * rows)
            back = contract_cols(gfs[m][...], wd[...])
            grad_g = (back * mul_g[at, :]).astype(BF)
            grad_u = (back * mul_u[at, :]).astype(BF)
            dg[at, :] = grad_g
            du[at, :] = grad_u
            part = dot_nn(grad_g, wg[...]) + dot_nn(grad_u, wu[...])
            parts[m][...] = part.astype(parts[m].dtype)

    def ffn_grads_kernel(ids, *refs):
        xs = refs[:cols]
        gfs = refs[cols : 2 * cols]
        hid, dg, du = refs[2 * cols : 2 * cols + 3]
        keep, send = refs[2 * cols + 3 : 2 * cols + 5]
        stack = refs[2 * cols + 5]
        for part, left, right in ((0, dg, xs), (1, du, xs), (2, hid, gfs)):
            for m in range(cols):
                stack[m * rows : (m + 1) * rows, :] = right[m][...]
            grad = contract_rows(left[...], stack[...])
            for k in range(chips):
                keep[k, part * ff_cut : (part + 1) * ff_cut, :] = grad[
                    k * ff_cut : (k + 1) * ff_cut, :
                ].astype(keep.dtype)
                send[k, part * ff_cut : (part + 1) * ff_cut, :] = grad[
                    (chips + k) * ff_cut : (chips + k + 1) * ff_cut, :
                ].astype(send.dtype)

    def mid_back_kernel(ids, *refs):
        parts = refs[:cols]
        mid, cot, attn_raw, gain_f, gain_pa, att = refs[cols : cols + 6]
        gmid_out, gab_out, keep, send, gf_gain, gpa_gain = refs[cols + 6 : cols + 12]
        go = refs[cols + 12]
        total = parts[0][...]
        for m in range(1, cols):
            total = total + parts[m][...].astype(F32)
        grad, gain_grad = norm_back_rows(total, mid[...], gain_f[...])
        gf_gain[...] = gain_grad
        gmid = cot[...] + grad
        gmid_out[...] = gmid
        grad, gain_grad = norm_back_rows(gmid, attn_raw[...], gain_pa[...])
        gpa_gain[...] = gain_grad
        gab = grad.astype(BF)
        gab_out[...] = gab
        go[...] = contract_rows(att[...], gab)
        for r, dest in ((0, keep), (1, send)):
            for m in range(cols):
                for k in range(chips):
                    base = shard_of(ids, r, k) * cols + (ids[0] ^ m)
                    at = pl.ds(aligned(base, q_cut), q_cut)
                    dest[m, k * q_cut : (k + 1) * q_cut, :] = go[at, :].astype(BF)

    def attend_back_kernel(ids, *refs):
        (gab, gain_q, wo, att, probs, q_rot, q_raw, k_all, v_all, cos_ref, sin_ref) = refs[:11]
        q_msgs = refs[11 : 11 + chips]
        keep, send, gq_gain = refs[11 + chips : 14 + chips]
        dot_b, ds, dkv, qgb = refs[14 + chips :]
        me = shard_of(ids, 0, 0)
        own = pl.ds(aligned(me, rows), rows)
        cosine, sine = cos_ref[own, :], sin_ref[own, :]
        gq_total = jnp.zeros((1, hd), F32)
        for n in range(heads):
            lanes = slice(n * hd, (n + 1) * hd)
            at = slice(n * rows, (n + 1) * rows)
            d_out = contract_cols(gab[...], wo[lanes, :]).astype(BF)
            dot_b[at, :] = d_out
            delta = jnp.sum(
                d_out.astype(F32) * att[:, lanes].astype(F32), axis=-1, keepdims=True
            )
            prob_grad = contract_cols(d_out, v_all[...])
            score_grad = (probs[at, :].astype(F32) * (prob_grad - delta)).astype(BF)
            ds[at, :] = score_grad
            q_grad = dot_nn(score_grad, k_all[...]) * score_scale
            q_grad, gain_grad = norm_back_rows(
                spin(q_grad, cosine, -sine), q_raw[:, lanes], gain_q[...]
            )
            gq_total = gq_total + gain_grad
            q_grad = q_grad.astype(BF)
            pair = 2 * q_own
            for i in range(n * hd // pair, (n + 1) * hd // pair):
                qgb[i] = q_grad[:, i * pair - n * hd : (i + 1) * pair - n * hd]
        gq_gain[...] = gq_total
        for k in range(chips):
            q_msgs[k][...] = qgb[ids[1] ^ k]
        dkv[:, :hd] = contract_rows(ds[...], q_rot[...]) * score_scale
        dkv[:, hd:] = contract_rows(probs[...], dot_b[...])
        for k in range(chips):
            at = pl.ds(aligned(shard_of(ids, 0, k), rows), rows)
            keep[k] = dkv[at, :].astype(BF)
            at = pl.ds(aligned(shard_of(ids, 1, k), rows), rows)
            send[k] = dkv[at, :].astype(BF)

    def pair_kernel(ids, keep, got, *outs):
        for k in range(chips):
            outs[k][...] = (keep[k].astype(F32) + got[k].astype(F32)).astype(outs[k].dtype)

    def query_dx_kernel(ids, *refs):
        wq, dx = refs[chips:]
        pair = 2 * q_own
        total = jnp.zeros((rows, dim), F32)
        for k in range(chips):
            at = pl.ds(aligned(ids[1] ^ k, pair), pair)
            total = total + dot_nn(refs[k][...], wq[at, :])
        dx[...] = total

    def split_kernel(ids, keep, got, *outs):
        for m in range(cols):
            outs[m][...] = (keep[m].astype(F32) + got[m].astype(F32)).astype(outs[m].dtype)

    def chip_sum_kernel(ids, *refs):
        total = refs[0][...].astype(F32)
        for k in range(1, chips):
            total = total + refs[k][...].astype(F32)
        refs[chips][...] = total.astype(BF)

    def key_back_kernel(ids, *refs):
        parts = refs[:chips]
        (k_raw, gain_k, wkv, dxq, tok, gain_attn, gmid, cos_ref, sin_ref) = refs[
            chips : chips + 9
        ]
        g_q, g_pa, g_f, g_pf, wide_e, wide_s, thin_e, thin_s = refs[chips + 9 : chips + 17]
        outs_in = refs[chips + 17 : chips + 17 + cols]
        msgs = refs[chips + 17 + cols : 2 * chips + 17 + cols]
        gin_out = refs[2 * chips + 17 + cols]
        hold, grads = refs[2 * chips + 18 + cols :]
        me = shard_of(ids, 0, 0)
        own = pl.ds(aligned(me, rows), rows)
        total = parts[0][...]
        for k in range(1, chips):
            total = total + parts[k][...].astype(F32)
        grad, g_k = norm_back_rows(
            spin(total[:, :hd], cos_ref[own, :], -sin_ref[own, :]), k_raw[...], gain_k[...]
        )
        kvb = jnp.concatenate([grad, total[:, hd:]], axis=-1).astype(BF)
        dx = dxq[...] + dot_nn(kvb, wkv[...])
        grad, g_a = norm_back_rows(dx, tok[...].astype(F32), gain_attn[...])
        gin_out[...] = gmid[...] + grad
        pair = 2 * kv_own
        for k in range(chips):
            hold[k] = kvb[:, k * pair : (k + 1) * pair]
        segment = lax.broadcasted_iota(jnp.int32, (shards, 1), 0)
        grads[...] = jnp.zeros(grads.shape, F32)
        for g, vec in enumerate((g_a, g_q[...], g_k, g_pa[...], g_f[...], g_pf[...])):
            expand, seg = (wide_e, wide_s) if gain_cuts[g] == gain_cuts[0] else (thin_e, thin_s)
            spread = jnp.where(seg[...] == segment, vec, 0.0).astype(BF)
            packed = contract_cols(spread, expand[...])
            for s in range(shards):
                grads[s, g : g + 1, :] = packed[s : s + 1, :]
        for k in range(chips):
            to = ids[1] ^ k
            msgs[k][:rows, :] = hold[to]
            msgs[k][rows : rows + 16, :] = jnp.concatenate(
                [grads[2 * to], grads[2 * to + 1]], axis=0
            ).astype(BF)
            mine = slice(k * q_cut, (k + 1) * q_cut)
            piece = outs_in[0][mine, :].astype(F32)
            for m in range(1, cols):
                piece = piece + outs_in[m][mine, :].astype(F32)
            piece = piece.astype(BF)
            for i in range(dim // 128):
                at = rows + 16 + i * q_cut
                msgs[k][at : at + q_cut, :] = piece[:, i * 128 : (i + 1) * 128]

    def last_grads_kernel(ids, *refs):
        msgs = refs[:shards]
        q_msgs = refs[shards : 2 * shards]
        xn_all, out, cat, turned = refs[2 * shards :]
        gain = jnp.zeros((16, 128), F32)
        pair_q = 2 * q_own
        for r in range(2):
            for k in range(chips):
                msg = msgs[r * chips + k]
                at = pl.ds(aligned(shard_of(ids, r, k), rows), rows)
                cat[at, :pair_q] = q_msgs[r * chips + k][...]
                cat[at, pair_q:] = msg[:rows, :]
                gain = gain + msg[rows : rows + 16, :].astype(F32)
        turned[...] = contract_rows(cat[...], xn_all[...])
        at = pl.ds(aligned(ids[2], q_own), q_own)
        out[:q_own, :] = turned[at, :].astype(BF)
        at = pl.ds(pl.multiple_of(pair_q + ids[2] * kv_own, kv_own), kv_own)
        out[q_own : q_own + kv_own, :] = turned[at, :].astype(BF)
        start = q_own + kv_own
        for i in range(dim // 128):
            at = rows + 16 + i * q_cut
            piece = msgs[0][at : at + q_cut, :].astype(F32)
            for k in range(1, chips):
                piece = piece + msgs[k][at : at + q_cut, :].astype(F32)
            out[start : start + q_cut, i * 128 : (i + 1) * 128] = piece.astype(BF)
        start += q_cut
        gain = jnp.where(ids[2] == 0, gain[:8, :], gain[8:, :])
        out[start:, :] = jnp.zeros((16, dim), BF)
        out[start:, :128] = jnp.concatenate([gain, jnp.zeros((8, 128), F32)], axis=0).astype(BF)

    def finish_kernel(ids, *refs):
        pieces = refs[:cols]
        out_q, out_o, out_kv, out_g = refs[cols : cols + 4]
        split = q_own + kv_own
        total = pieces[0][:split, :].astype(F32)
        gain = pieces[0][split + q_cut :, :128].astype(F32)
        for m in range(1, cols):
            total = total + pieces[m][:split, :].astype(F32)
            gain = gain + pieces[m][split + q_cut :, :128].astype(F32)
        for m in range(cols):
            at = pl.ds(aligned(ids[0] ^ m, q_cut), q_cut)
            out_o[at, :] = pieces[m][split : split + q_cut, :].astype(F32)
        out_q[...] = total[:q_own, :].T
        out_kv[...] = total[q_own:, :]
        out_g[...] = gain[:8, :]

    def place_kernel(spec, ids, *refs):
        pieces = refs[:cols]
        outs = refs[cols : cols + len(spec)]
        holds = refs[cols + len(spec) :]
        start = 0
        for (cut, turned), out, hold in zip(spec, outs, holds):
            for m in range(cols):
                hold[pl.ds(aligned(ids[0] ^ m, cut), cut), :] = pieces[m][
                    start : start + cut, :
                ].astype(F32)
            out[...] = hold[...].T if turned else hold[...]
            start += cut

    def place(ids, pieces, spec):
        outs = [
            ((dim, cut * cols) if turned else (cut * cols, dim), F32) for cut, turned in spec
        ]
        scratch = [pltpu.VMEM((cut * cols, dim), F32) for cut, _ in spec]
        return run_block(functools.partial(place_kernel, spec), outs, ids, *pieces, scratch=scratch)

    def both(x, y):
        return lax.optimization_barrier((x, y))

    def fast_body(
        tokens,
        attn_norm,
        query_norm,
        key_norm,
        post_attn_norm,
        ffn_norm,
        post_ffn_norm,
        query_weight,
        keyval_weight,
        out_weight,
        gate_weight,
        up_weight,
        down_weight,
        cotangent,
    ):
        me_h = lax.axis_index("head").astype(jnp.int32)
        me_s = lax.axis_index("shard").astype(jnp.int32)
        ids = jnp.stack([me_h, me_s // 2, me_s % 2])
        tok, cot = tokens[0], cotangent[0]

        gains_own = jnp.stack(
            [
                jnp.pad(g.astype(F32), (0, 128 - g.shape[0]))
                for g in (attn_norm, query_norm, key_norm, post_attn_norm, ffn_norm, post_ffn_norm)
            ]
            + [jnp.zeros((128,), F32)] * 2
        )
        (pack_qkv,) = run_block(
            pack_qkv_kernel,
            [((qkv_cut, dim), BF)],
            ids,
            query_weight,
            keyval_weight.T,
            scratch=[pltpu.VMEM((q_own, dim), F32), pltpu.VMEM((kv_own, dim), F32)],
        )
        (pack_out,) = run_block(
            pack_out_kernel, [((q_cut + 16, dim), BF)], ids, out_weight, gains_own
        )
        (pack_ffn,) = run_block(
            pack_ffn_kernel,
            [((3 * ff_cut, dim), BF)],
            ids,
            gate_weight,
            up_weight,
            down_weight,
            scratch=[pltpu.VMEM((ff_own, dim), F32)],
        )
        qkv_z = all_along(pack_qkv)
        tok_z = all_along(tok)
        qkv_z = jnp.concatenate(qkv_z, axis=0)
        qkv_h = with_partner(all_across(qkv_z))
        toks = with_partner(tok_z)
        pack_out, _ = both(pack_out, qkv_z)
        out_z, gain_block = run_block(
            stage_out_kernel,
            [((chips * q_cut, dim), BF), ((chips * 16, 128), BF)],
            ids,
            *all_along(pack_out),
        )

        def spread_tables(width):
            cut = width // shards
            lane = jnp.arange(width, dtype=jnp.int32)[None, :]
            within = jnp.arange(128, dtype=jnp.int32)[:, None]
            return (lane % cut == within).astype(BF), lane // cut

        wide_e, wide_s = spread_tables(dim)
        thin_e, thin_s = spread_tables(hd)
        gain_attn, gain_q, gain_k, gain_pa, gain_f, gain_pf = run_block(
            gains_kernel,
            [((1, cut * shards), F32) for cut in gain_cuts],
            ids,
            gain_block,
            swap(gain_block),
            wide_e,
            wide_s,
            thin_e,
            thin_s,
        )
        out_h = all_across(out_z)
        pack_ffn, _ = both(pack_ffn, (tok_z, out_z))
        ffn_z = all_along(pack_ffn)

        half = hd // 2
        freqs = jnp.exp(
            jnp.arange(half, dtype=F32) * (-2.0 * math.log(rope_base) / hd)
        )
        angles = jnp.arange(length, dtype=jnp.int32).astype(F32)[:, None] * freqs
        cos_all, sin_all = jnp.cos(angles), jnp.sin(angles)

        _, wq, wkv, q_rot, k_all, v_all, q_raw, k_raw, probs, att, xn_all = run_block(
            attend_kernel,
            [
                ((rows, dim), BF),
                ((q_all, dim), BF),
                ((kv_all, dim), BF),
                ((heads * rows, hd), BF),
                ((length, hd), BF),
                ((length, hd), BF),
                ((rows, q_all), F32),
                ((rows, hd), F32),
                ((heads * rows, length), BF),
                ((rows, q_all), BF),
                ((length, dim), BF),
            ],
            ids,
            *toks,
            *qkv_h,
            gain_attn,
            gain_q,
            gain_k,
            cos_all,
            sin_all,
        )
        att, out_h = both(att, out_h)
        out_h = with_partner(out_h)
        wo, attn_raw, mid, xm = run_block(
            out_kernel,
            [((q_all, dim), BF), ((rows, dim), F32), ((rows, dim), F32), ((rows, dim), BF)],
            ids,
            att,
            tok,
            gain_pa,
            gain_f,
            *out_h,
        )
        xs = all_across(xm)
        ffn_z, _ = both(ffn_z, xm)
        ffn_packs = with_partner(ffn_z)
        ff_w = ((ff_local, dim), BF)
        part_outs = [((rows, dim), F32)] + [((rows, dim), BF)] * (cols - 1)
        wg, wu, wd, hid, mul_g, mul_u, *parts = run_block(
            ffn_kernel,
            [ff_w, ff_w, ff_w, ((cols * rows, ff_local), BF)]
            + [((cols * rows, ff_local), F32)] * 2
            + part_outs,
            ids,
            *xs,
            *ffn_packs,
        )
        parts = trade_across(parts)
        out, gf, g_pf = run_block(
            head_out_kernel,
            [((rows, dim), F32), ((rows, dim), BF), ((1, dim), F32)],
            ids,
            *parts,
            mid,
            cot,
            gain_pf,
        )
        gfs = all_across(gf)
        dg, du, *parts = run_block(
            ffn_back_kernel,
            [((cols * rows, ff_local), BF)] * 2 + part_outs,
            ids,
            *gfs,
            wg,
            wu,
            wd,
            mul_g,
            mul_u,
        )
        parts = trade_across(parts)
        keep, send = run_block(
            ffn_grads_kernel,
            [((chips, 3 * ff_cut, dim), BF), ((chips, 3 * ff_cut, dim), BF)],
            ids,
            *xs,
            *gfs,
            hid,
            dg,
            du,
            scratch=[pltpu.VMEM((cols * rows, dim), BF)],
        )
        parts, keep, send = lax.optimization_barrier((parts, keep, send))
        got = swap(send)
        ff_piece = (3 * ff_cut, dim)
        mine = run_block(
            pair_kernel, [(ff_piece, F32)] + [(ff_piece, BF)] * (chips - 1), ids, keep, got
        )
        parts, mine = both(parts, mine)
        ff_parts = trade_along(mine)
        (ff_sum,) = run_block(chip_sum_kernel, [(ff_piece, BF)], ids, *ff_parts)
        gmid, gab, keep, send, g_f, g_pa = run_block(
            mid_back_kernel,
            [
                ((rows, dim), F32),
                ((rows, dim), BF),
                ((cols, chips * q_cut, dim), BF),
                ((cols, chips * q_cut, dim), BF),
                ((1, dim), F32),
                ((1, dim), F32),
            ],
            ids,
            *parts,
            mid,
            cot,
            attn_raw,
            gain_f,
            gain_pa,
            att,
            scratch=[pltpu.VMEM((q_all, dim), F32)],
        )
        got = swap(send)
        out_split = ((chips * q_cut, dim), BF)
        out_parts = run_block(split_kernel, [out_split] * cols, ids, keep, got)
        out_parts = trade_across(out_parts)

        *q_msgs, keep, send, g_q = run_block(
            attend_back_kernel,
            [((rows, 2 * q_own), BF)] * chips
            + [((chips, rows, kv_all), BF), ((chips, rows, kv_all), BF), ((1, hd), F32)],
            ids,
            gab,
            gain_q,
            wo,
            att,
            probs,
            q_rot,
            q_raw,
            k_all,
            v_all,
            cos_all,
            sin_all,
            scratch=[
                pltpu.VMEM((heads * rows, hd), BF),
                pltpu.VMEM((heads * rows, length), BF),
                pltpu.VMEM((length, kv_all), F32),
                pltpu.VMEM((chips, rows, 2 * q_own), BF),
            ],
        )
        got = swap(send)
        kv_piece = (rows, kv_all)
        mine = run_block(
            pair_kernel, [(kv_piece, F32)] + [(kv_piece, BF)] * (chips - 1), ids, keep, got
        )
        kv_parts = trade_along(mine)
        (dxq,) = run_block(query_dx_kernel, [((rows, dim), F32)], ids, *q_msgs, wq)
        q_msgs = with_partner(trade_along(q_msgs))
        kv_parts, ff_sum = both(kv_parts, ff_sum)
        *msgs, grad_input = run_block(
            key_back_kernel,
            [((rows + 16 + q_cut * dim // 128, 2 * kv_own), BF)] * chips + [((rows, dim), F32)],
            ids,
            *kv_parts,
            k_raw,
            gain_k,
            wkv,
            dxq,
            tok,
            gain_attn,
            gmid,
            cos_all,
            sin_all,
            g_q,
            g_pa,
            g_f,
            g_pf,
            wide_e,
            wide_s,
            thin_e,
            thin_s,
            *out_parts,
            scratch=[
                pltpu.VMEM((chips, rows, 2 * kv_own), BF),
                pltpu.VMEM((shards, 8, 128), F32),
            ],
        )
        msgs = trade_along(msgs)
        ff_sum, _ = both(ff_sum, grad_input)
        ff_pieces = all_across(ff_sum)
        msgs = with_partner(msgs)
        last = (q_own + kv_own + q_cut + 16, dim)
        both_cols = 2 * (q_own + kv_own)
        (piece,) = run_block(
            last_grads_kernel,
            [(last, BF)],
            ids,
            *msgs,
            *q_msgs,
            xn_all,
            scratch=[pltpu.VMEM((length, both_cols), BF), pltpu.VMEM((both_cols, dim), F32)],
        )
        ff_pieces, _ = both(ff_pieces, piece)
        grad_gate, grad_up, grad_down = place(
            ids, ff_pieces, ((ff_cut, True), (ff_cut, True), (ff_cut, False))
        )
        pieces = all_across(piece)
        grad_query_w, grad_out, grad_keyval_w, gain_own = run_block(
            finish_kernel,
            [
                ((dim, q_own), F32),
                ((q_own, dim), F32),
                ((kv_own, dim), F32),
                ((8, 128), F32),
            ],
            ids,
            *pieces,
        )
        grad_keyval_w = grad_keyval_w.T
        small = [gain_own[g, :cut] for g, cut in enumerate(gain_cuts)]
        return (
            out[None],
            grad_input[None],
            *small,
            grad_query_w,
            grad_keyval_w,
            grad_out,
            grad_gate,
            grad_up,
            grad_down,
        )

    return fast_body


def power_of_two(number):
    return number & (number - 1) == 0


def direct_fits(mesh, tokens, query_weight, keyval_weight, gate_weight):
    cols, shards = mesh.shape["head"], mesh.shape["shard"]
    parts = cols * shards
    return (
        power_of_two(cols)
        and power_of_two(shards)
        and cols <= 4
        and 2 <= shards <= 8
        and tokens.shape[1] <= 1024
        and tokens.shape[2] % 128 == 0
        and tokens.shape[1] % (16 * shards) == 0
        and keyval_weight.shape[1] % 512 == 0
        and tokens.shape[2] <= 128 * shards
        and keyval_weight.shape[1] == 64 * shards
        and all(w.shape[1] % (16 * parts) == 0 for w in (query_weight, keyval_weight, gate_weight))
    )


def solution(mesh):
    placed = (
        P("head", "shard", None),
        P("shard"),
        P("shard"),
        P("shard"),
        P("shard"),
        P("shard"),
        P("shard"),
        P(None, "shard"),
        P(None, "shard"),
        P("shard", None),
        P(None, "shard"),
        P(None, "shard"),
        P("shard", None),
        P("head", "shard", None),
    )

    def run(*args):
        tokens, query_weight, keyval_weight, gate_weight = args[0], args[7], args[8], args[10]
        inner = body
        if direct_fits(mesh, tokens, query_weight, keyval_weight, gate_weight):
            widths = (query_weight.shape[1], keyval_weight.shape[1], gate_weight.shape[1])
            inner = make_fast(mesh, tokens.shape, widths)
        return jax.shard_map(
            inner,
            mesh=mesh,
            in_specs=placed,
            out_specs=(
                P("head", "shard", None),
                P("head", "shard", None),
                P("shard"),
                P("shard"),
                P("shard"),
                P("shard"),
                P("shard"),
                P("shard"),
                P(None, "shard"),
                P(None, "shard"),
                P("shard", None),
                P(None, "shard"),
                P(None, "shard"),
                P("shard", None),
            ),
            check_vma=False,
        )(*args)

    return run
```

```python
import functools
import math

import jax
import jax.numpy as jnp
from jax import lax
from jax.experimental import pallas as pl
from jax.experimental.pallas import tpu as pltpu
from jax.sharding import PartitionSpec as P

HEADS = 4
HD = 256


norm_eps = 1e-06
rope_base = 1000000.0
score_scale = 0.0625
gelu_coef = 0.7978845608028654


def rms_scale(values):
    return lax.rsqrt(jnp.mean(values * values, axis=-1, keepdims=True) + norm_eps)


def norm_back(upstream, values, gain):
    scale = rms_scale(values)
    weighted = upstream * gain
    inner = jnp.mean(weighted * values, axis=-1, keepdims=True)
    grad_values = scale * weighted - values * (scale * scale * scale) * inner
    leading = tuple(range(values.ndim - 1))
    grad_gain = jnp.sum(upstream * values * scale, axis=leading)
    return (grad_values, grad_gain)


def rotate(values, positions, direction):
    half = values.shape[-1] // 2
    index = jnp.arange(half, dtype=jnp.float32)
    freqs = jnp.exp(index * (-2.0 * math.log(rope_base) / values.shape[-1]))
    angles = positions.astype(jnp.float32)[..., None] * freqs
    cosine = jnp.cos(angles)
    sine = direction * jnp.sin(angles)
    first = values[..., :half]
    second = values[..., half:]
    return jnp.concatenate(
        [first * cosine - second * sine, second * cosine + first * sine], axis=-1
    )


def gelu_parts(values):
    inner = gelu_coef * (values + 0.044715 * values * values * values)
    tanh_value = jnp.tanh(inner)
    value = 0.5 * values * (1.0 + tanh_value)
    slope = 0.5 * (1.0 + tanh_value) + 0.5 * values * (
        1.0 - tanh_value * tanh_value
    ) * gelu_coef * (1.0 + 3.0 * 0.044715 * values * values)
    return (value, slope)


def contract_rows(left, right):
    return lax.dot_general(
        left, right, (((0,), (0,)), ((), ())), preferred_element_type=jnp.float32
    )


def contract_cols(left, right):
    return lax.dot_general(
        left, right, (((1,), (1,)), ((), ())), preferred_element_type=jnp.float32
    )


def masked_scores(queries, keys, query_pos, key_start):
    scores = (
        jnp.einsum("gid,gjd->gij", queries, keys, preferred_element_type=jnp.float32) * score_scale
    )
    key_pos = key_start + jnp.arange(keys.shape[1], dtype=jnp.int32)
    allowed = query_pos[:, None] >= key_pos[None, :]
    return (jnp.where(allowed[None], scores, -1e30), allowed)


def sweep_tiles(visit, state, piece, last_pos):
    count = piece.shape[1]
    tile = math.gcd(count, 2048)
    number = count // tile

    def sweep_step_tile(index, current):
        offset = index * tile
        tile_data = lax.dynamic_slice_in_dim(piece, index * tile, tile, 1)
        return lax.cond(
            offset <= last_pos,
            lambda held: visit(held, tile_data, offset),
            lambda held: held,
            current,
        )

    return lax.fori_loop(0, number, sweep_step_tile, state)


def body(
    tokens,
    attn_norm,
    query_norm,
    key_norm,
    post_attn_norm,
    ffn_norm,
    post_ffn_norm,
    query_weight,
    keyval_weight,
    out_weight,
    gate_weight,
    up_weight,
    down_weight,
    cotangent,
):
    gathered = (
        lax.all_gather(attn_norm, "shard", axis=0, tiled=True),
        lax.all_gather(query_norm, "shard", axis=0, tiled=True),
        lax.all_gather(key_norm, "shard", axis=0, tiled=True),
        lax.all_gather(post_attn_norm, "shard", axis=0, tiled=True),
        lax.all_gather(ffn_norm, "shard", axis=0, tiled=True),
        lax.all_gather(post_ffn_norm, "shard", axis=0, tiled=True),
        lax.all_gather(query_weight, "shard", axis=1, tiled=True),
        lax.all_gather(keyval_weight, "shard", axis=1, tiled=True),
        lax.all_gather(out_weight, "shard", axis=0, tiled=True),
        lax.all_gather(gate_weight, "shard", axis=1, tiled=True),
        lax.all_gather(up_weight, "shard", axis=1, tiled=True),
        lax.all_gather(down_weight, "shard", axis=0, tiled=True),
    )
    gain_attn, gain_query, gain_key, gain_post_attn, gain_ffn, gain_post_ffn = [
        g.astype(jnp.float32) for g in gathered[:6]
    ]
    full_query, full_keyval, full_out, full_gate, full_up, full_down = gathered[6:]
    back_query, back_keyval, back_out, back_gate, back_up, back_down = gathered[6:]
    rows = tokens.shape[1]
    positions = lax.axis_index("shard") * rows + jnp.arange(rows, dtype=jnp.int32)
    first_pos = positions[0]
    last_pos = positions[rows - 1]
    residual_in = tokens[0].astype(jnp.float32)
    normed_in = (residual_in * rms_scale(residual_in) * gain_attn).astype(jnp.bfloat16)
    query_raw = jnp.dot(normed_in, full_query, preferred_element_type=jnp.float32).reshape(
        rows, HEADS, HD
    )
    keyval_raw = jnp.dot(normed_in, full_keyval, preferred_element_type=jnp.float32)
    key_raw = keyval_raw[:, :HD]
    query_rot = rotate(
        query_raw * rms_scale(query_raw) * gain_query, positions[:, None], 1.0
    ).astype(jnp.bfloat16)
    key_rot = rotate(key_raw * rms_scale(key_raw) * gain_key, positions, 1.0).astype(jnp.bfloat16)
    keyval_rot = jnp.concatenate([key_rot, keyval_raw[:, HD:].astype(jnp.bfloat16)], axis=-1)
    query_heads_first = jnp.transpose(query_rot, (1, 0, 2))
    keyval_copies = jnp.broadcast_to(keyval_rot[None], (HEADS, rows, 2 * HD))
    head_queries, head_keyvals = (
        lax.all_to_all(query_heads_first, "head", split_axis=0, concat_axis=0, tiled=True),
        lax.all_to_all(keyval_copies, "head", split_axis=0, concat_axis=0, tiled=True),
    )
    seq_count = head_queries.shape[0]

    def online_tile(state, tile_data, offset):
        running_max, running_sum, weighted = state
        scores, allowed = masked_scores(head_queries, tile_data[:, :, :HD], positions, offset)
        new_max = jnp.maximum(running_max, jnp.max(scores, axis=-1))
        probs = jnp.where(allowed[None], jnp.exp(scores - new_max[..., None]), 0.0)
        fade = jnp.exp(running_max - new_max)
        running_sum = running_sum * fade + jnp.sum(probs, axis=-1)
        weighted = weighted * fade[..., None] + jnp.einsum(
            "gij,gjd->gid",
            probs.astype(jnp.bfloat16),
            tile_data[:, :, HD:],
            preferred_element_type=jnp.float32,
        )
        return (new_max, running_sum, weighted)

    start_state = (
        jnp.full((seq_count, rows), -1e30, jnp.float32),
        jnp.zeros((seq_count, rows), jnp.float32),
        jnp.zeros((seq_count, rows, HD), jnp.float32),
    )
    all_keyvals = lax.all_gather(head_keyvals, "shard", axis=1, tiled=True)
    final_state = sweep_tiles(online_tile, start_state, all_keyvals, last_pos)
    top_score, total_weight, weighted_sum = final_state
    attended = (weighted_sum / total_weight[..., None]).astype(jnp.bfloat16)
    log_norm = top_score + jnp.log(total_weight)
    returned = lax.all_to_all(attended, "head", split_axis=0, concat_axis=0, tiled=True)
    own_heads = jnp.transpose(returned, (1, 0, 2)).reshape(rows, HEADS * HD)
    attn_raw = jnp.dot(own_heads, full_out, preferred_element_type=jnp.float32)
    residual_mid = residual_in + attn_raw * rms_scale(attn_raw) * gain_post_attn
    normed_mid = (residual_mid * rms_scale(residual_mid) * gain_ffn).astype(jnp.bfloat16)
    gate_raw = jnp.dot(normed_mid, full_gate, preferred_element_type=jnp.float32)
    up_raw = jnp.dot(normed_mid, full_up, preferred_element_type=jnp.float32)
    gelu_value, gelu_slope = gelu_parts(gate_raw)
    hidden = (gelu_value * up_raw).astype(jnp.bfloat16)
    ffn_raw = jnp.dot(hidden, full_down, preferred_element_type=jnp.float32)
    result = residual_mid + ffn_raw * rms_scale(ffn_raw) * gain_post_ffn
    upstream = cotangent[0]
    grad_ffn_raw, grad_post_ffn = norm_back(upstream, ffn_raw, gain_post_ffn)
    grad_ffn_b = grad_ffn_raw.astype(jnp.bfloat16)
    grad_down = contract_rows(hidden, grad_ffn_b)
    grad_hidden = contract_cols(grad_ffn_b, back_down)
    grad_gate_b = (grad_hidden * up_raw * gelu_slope).astype(jnp.bfloat16)
    grad_up_b = (grad_hidden * gelu_value).astype(jnp.bfloat16)
    grad_gate = contract_rows(normed_mid, grad_gate_b)
    grad_up = contract_rows(normed_mid, grad_up_b)
    grad_normed_mid = contract_cols(grad_gate_b, back_gate) + contract_cols(grad_up_b, back_up)
    grad_mid_part, grad_ffn_gain = norm_back(grad_normed_mid, residual_mid, gain_ffn)
    grad_mid = upstream + grad_mid_part
    grad_attn_raw, grad_post_attn = norm_back(grad_mid, attn_raw, gain_post_attn)
    grad_attn_b = grad_attn_raw.astype(jnp.bfloat16)
    grad_out = contract_rows(own_heads, grad_attn_b)
    heads_grad_b = (
        contract_cols(grad_attn_b, back_out).astype(jnp.bfloat16).reshape(rows, HEADS, HD)
    )
    head_grads = lax.all_to_all(
        jnp.transpose(heads_grad_b, (1, 0, 2)), "head", split_axis=0, concat_axis=0, tiled=True
    )
    delta = jnp.sum(head_grads.astype(jnp.float32) * attended.astype(jnp.float32), axis=-1)

    def score_parts(tile_data, offset):
        scores, _ = masked_scores(head_queries, tile_data[:, :, :HD], positions, offset)
        probs = jnp.exp(scores - log_norm[..., None])
        prob_grad = jnp.einsum(
            "gid,gjd->gij", head_grads, tile_data[:, :, HD:], preferred_element_type=jnp.float32
        )
        score_grad = (probs * (prob_grad - delta[..., None])).astype(jnp.bfloat16)
        return (probs, score_grad)

    def query_tile(query_sum, tile_data, offset):
        _, score_grad = score_parts(tile_data, offset)
        return (
            query_sum
            + jnp.einsum(
                "gij,gjd->gid", score_grad, tile_data[:, :, :HD], preferred_element_type=jnp.float32
            )
            * score_scale
        )

    grad_queries = sweep_tiles(
        query_tile, jnp.zeros((seq_count, rows, HD), jnp.float32), all_keyvals, last_pos
    )
    all_logs, all_deltas = (
        lax.all_gather(log_norm, "shard", axis=1, tiled=True),
        lax.all_gather(delta, "shard", axis=1, tiled=True),
    )
    own_keys = head_keyvals[:, :, :HD]
    own_values = head_keyvals[:, :, HD:]
    query_piece = lax.all_gather(head_queries, "shard", axis=1, tiled=True)
    grad_piece = lax.all_gather(head_grads, "shard", axis=1, tiled=True)
    count = query_piece.shape[1]
    tile = math.gcd(count, 2048)
    number = count // tile

    def later_step_tile(index, current):
        offset = index * tile
        query_tile_data = lax.dynamic_slice_in_dim(query_piece, index * tile, tile, 1)
        grad_tile_data = lax.dynamic_slice_in_dim(grad_piece, index * tile, tile, 1)

        def compute(held):
            query_pos = offset + jnp.arange(tile, dtype=jnp.int32)
            logs = lax.dynamic_slice_in_dim(all_logs, offset, tile, 1)
            deltas = lax.dynamic_slice_in_dim(all_deltas, offset, tile, 1)
            scores, _ = masked_scores(query_tile_data, own_keys, query_pos, first_pos)
            probs = jnp.exp(scores - logs[..., None])
            prob_grad = jnp.einsum(
                "gid,gjd->gij", grad_tile_data, own_values, preferred_element_type=jnp.float32
            )
            score_grad = (probs * (prob_grad - deltas[..., None])).astype(jnp.bfloat16)
            key_part = (
                jnp.einsum(
                    "gij,gid->gjd", score_grad, query_tile_data, preferred_element_type=jnp.float32
                )
                * score_scale
            )
            value_part = jnp.einsum(
                "gij,gid->gjd",
                probs.astype(jnp.bfloat16),
                grad_tile_data,
                preferred_element_type=jnp.float32,
            )
            return held + jnp.concatenate([key_part, value_part], axis=-1)

        return lax.cond(offset + tile - 1 >= first_pos, compute, lambda held: held, current)

    key_grads = lax.fori_loop(
        0, number, later_step_tile, jnp.zeros((seq_count, rows, 2 * HD), jnp.float32)
    )
    query_back, keyval_back = (
        lax.all_to_all(
            grad_queries.astype(jnp.bfloat16), "head", split_axis=0, concat_axis=0, tiled=True
        ).astype(grad_queries.dtype),
        lax.all_to_all(
            key_grads.astype(jnp.bfloat16), "head", split_axis=0, concat_axis=0, tiled=True
        ).astype(key_grads.dtype),
    )
    query_back = jnp.transpose(query_back, (1, 0, 2))
    keyval_sum = jnp.sum(keyval_back, axis=0)
    grad_query_raw, grad_query_gain = norm_back(
        rotate(query_back, positions[:, None], -1.0), query_raw, gain_query
    )
    grad_key_raw, grad_key_gain = norm_back(
        rotate(keyval_sum[:, :HD], positions, -1.0), key_raw, gain_key
    )
    grad_query_b = grad_query_raw.reshape(rows, HEADS * HD).astype(jnp.bfloat16)
    grad_keyval_b = jnp.concatenate([grad_key_raw, keyval_sum[:, HD:]], axis=-1).astype(
        jnp.bfloat16
    )
    grad_query_w = contract_rows(normed_in, grad_query_b)
    grad_keyval_w = contract_rows(normed_in, grad_keyval_b)
    grad_normed_in = contract_cols(grad_query_b, back_query) + contract_cols(
        grad_keyval_b, back_keyval
    )
    grad_in_part, grad_attn_gain = norm_back(grad_normed_in, residual_in, gain_attn)
    grad_input = grad_mid + grad_in_part
    summed = (
        lax.psum_scatter(grad_attn_gain, "shard", scatter_dimension=0, tiled=True),
        lax.psum_scatter(grad_query_gain, "shard", scatter_dimension=0, tiled=True),
        lax.psum_scatter(grad_key_gain, "shard", scatter_dimension=0, tiled=True),
        lax.psum_scatter(grad_post_attn, "shard", scatter_dimension=0, tiled=True),
        lax.psum_scatter(grad_ffn_gain, "shard", scatter_dimension=0, tiled=True),
        lax.psum_scatter(grad_post_ffn, "shard", scatter_dimension=0, tiled=True),
        lax.psum_scatter(grad_query_w, "shard", scatter_dimension=1, tiled=True),
        lax.psum_scatter(grad_keyval_w, "shard", scatter_dimension=1, tiled=True),
        lax.psum_scatter(grad_out, "shard", scatter_dimension=0, tiled=True),
        lax.psum_scatter(grad_gate, "shard", scatter_dimension=1, tiled=True),
        lax.psum_scatter(grad_up, "shard", scatter_dimension=1, tiled=True),
        lax.psum_scatter(grad_down, "shard", scatter_dimension=0, tiled=True),
    )
    summed = (
        lax.psum(summed[0].astype(jnp.bfloat16), "head").astype(jnp.float32),
        lax.psum(summed[1].astype(jnp.bfloat16), "head").astype(jnp.float32),
        lax.psum(summed[2].astype(jnp.bfloat16), "head").astype(jnp.float32),
        lax.psum(summed[3].astype(jnp.bfloat16), "head").astype(jnp.float32),
        lax.psum(summed[4].astype(jnp.bfloat16), "head").astype(jnp.float32),
        lax.psum(summed[5].astype(jnp.bfloat16), "head").astype(jnp.float32),
        lax.psum(summed[6].astype(jnp.bfloat16), "head").astype(jnp.float32),
        lax.psum(summed[7].astype(jnp.bfloat16), "head").astype(jnp.float32),
        lax.psum(summed[8].astype(jnp.bfloat16), "head").astype(jnp.float32),
        lax.psum(summed[9].astype(jnp.bfloat16), "head").astype(jnp.float32),
        lax.psum(summed[10].astype(jnp.bfloat16), "head").astype(jnp.float32),
        lax.psum(summed[11].astype(jnp.bfloat16), "head").astype(jnp.float32),
    )
    return (
        result[None],
        grad_input[None],
        summed[0],
        summed[1],
        summed[2],
        summed[3],
        summed[4],
        summed[5],
        summed[6],
        summed[7],
        summed[8],
        summed[9],
        summed[10],
        summed[11],
    )


BF = jnp.bfloat16
F32 = jnp.float32
MIB = 1024 * 1024


def dot_nn(left, right):
    return lax.dot_general(
        left, right, (((1,), (0,)), ((), ())), preferred_element_type=jnp.float32
    )


def rms_inv(values):
    return lax.rsqrt(jnp.mean(values * values, axis=-1, keepdims=True) + norm_eps)


def norm_back_rows(upstream, values, gain):
    scale = rms_inv(values)
    weighted = upstream * gain
    inner = jnp.mean(weighted * values, axis=-1, keepdims=True)
    grad_values = scale * weighted - values * (scale * scale * scale) * inner
    grad_gain = jnp.sum(upstream * values * scale, axis=0, keepdims=True)
    return grad_values, grad_gain


def spin(values, cosine, sine):
    half = values.shape[-1] // 2
    first = values[:, :half]
    second = values[:, half:]
    return jnp.concatenate(
        [first * cosine - second * sine, second * cosine + first * sine], axis=-1
    )


def padded_bytes(shape, kind):
    size = jnp.dtype(kind).itemsize
    shape = (1, 1) + tuple(shape)
    return math.prod(shape[:-2]) * max(shape[-2], 16) * max(shape[-1], 128) * size


def run_block(kernel, outs, ids, *args, scratch=(), slack=4, space=pltpu.VMEM):
    held = sum(padded_bytes(x.shape, x.dtype) for x in args)
    held += sum(padded_bytes(shape, kind) for shape, kind in outs)
    held += sum(padded_bytes(x.shape, x.dtype) for x in scratch if isinstance(x.dtype, jnp.dtype))
    return pl.pallas_call(
        kernel,
        out_shape=[jax.ShapeDtypeStruct(shape, kind) for shape, kind in outs],
        in_specs=[pl.BlockSpec(memory_space=pltpu.SMEM)]
        + [pl.BlockSpec(memory_space=space)] * len(args),
        out_specs=[pl.BlockSpec(memory_space=pltpu.VMEM)] * len(outs),
        scratch_shapes=list(scratch),
        compiler_params=pltpu.CompilerParams(vmem_limit_bytes=held + slack * MIB),
    )(ids, *args)


def aligned(start, step):
    return pl.multiple_of(start * step, step)


def make_fast(mesh, tokens_shape, widths):
    cols = mesh.shape["head"]
    shards = mesh.shape["shard"]
    chips = shards // 2
    length, dim = tokens_shape[1], tokens_shape[2]
    q_all, kv_all, ff_all = widths
    hd = kv_all // 2
    heads = q_all // hd
    rows = length // shards
    q_own, kv_own, ff_own = q_all // shards, kv_all // shards, ff_all // shards
    q_cut, kv_cut, ff_cut = q_own // cols, kv_own // cols, ff_own // cols
    ff_local = ff_cut * shards
    qkv_cut = q_cut + kv_cut
    qo_cut = 2 * q_cut
    gain_cuts = (dim // shards, hd // shards, hd // shards) + (dim // shards,) * 3

    def swap(x):
        return lax.ppermute(x, "shard", [(s, s ^ 1) for s in range(shards)])

    def along(x, k):
        return lax.ppermute(x, "shard", [(s, s ^ (2 * k)) for s in range(shards)])

    def across(x, m):
        return lax.ppermute(x, "head", [(h, h ^ m) for h in range(cols)])

    def all_along(x):
        parts = [x]
        if chips > 2:
            far = along(x, 2)
        if chips > 1:
            parts.append(along(x, 1))
        if chips > 2:
            parts += [far, lax.ppermute(far, "shard", [(s, s ^ 2) for s in range(shards)])]
        return parts

    def all_across(x):
        return [x] + [across(x, m) for m in range(1, cols)]

    def trade_along(xs):
        return [xs[0]] + [along(xs[k], k) for k in range(1, chips)]

    def trade_across(xs):
        return [xs[0]] + [across(xs[m], m) for m in range(1, cols)]

    def with_partner(xs):
        return list(xs) + [swap(x) for x in xs]

    def shard_of(ids, r, k):
        return (ids[1] ^ k) * 2 + (ids[2] ^ r)

    def pack_qkv_kernel(ids, *refs):
        count = 2 + len(gain_cuts)
        far, (out, whole), sems = refs[:count], refs[count : count + 2], refs[-1]
        near = refs[count + 2 : 2 * count + 2]
        hold_q, hold_kv, hold_g = refs[2 * count + 2 : -1]
        copies = [pltpu.make_async_copy(f, n, sems.at[i]) for i, (f, n) in enumerate(zip(far, near))]
        for copy in copies:
            copy.start()
        hold_g[...] = jnp.zeros(hold_g.shape, F32)
        out[qkv_cut:, :] = jnp.zeros((16, dim), BF)
        for copy in copies:
            copy.wait()
        hold_q[...] = near[0][...].astype(F32).T
        hold_kv[...] = near[1][...].astype(F32)
        whole[:q_own, :] = hold_q[...].astype(BF)
        whole[q_own:, :] = near[1][...]
        for g, (gain, cut) in enumerate(zip(near[2:], gain_cuts)):
            hold_g[g : g + 1, :cut] = gain[...].astype(F32).reshape(1, cut)
        out[:q_cut, :] = hold_q[pl.ds(aligned(ids[0], q_cut), q_cut), :].astype(BF)
        out[q_cut:qkv_cut, :] = hold_kv[pl.ds(aligned(ids[0], kv_cut), kv_cut), :].astype(BF)
        out[qkv_cut:, :128] = hold_g[...].astype(BF)

    def pack_ffn_kernel(ids, far_g, far_u, far_d, out, near_g, near_u, near_d, hold, sems):
        at = pl.ds(aligned(ids[0], ff_cut), ff_cut)
        copies = [
            pltpu.make_async_copy(far_g, near_g, sems.at[0]),
            pltpu.make_async_copy(far_u, near_u, sems.at[1]),
            pltpu.make_async_copy(far_d.at[at, :], near_d, sems.at[2]),
        ]
        for copy in copies:
            copy.start()
        copies[0].wait()
        hold[...] = near_g[...].astype(F32).T
        out[:ff_cut, :] = hold[at, :].astype(BF)
        copies[1].wait()
        hold[...] = near_u[...].astype(F32).T
        out[ff_cut : 2 * ff_cut, :] = hold[at, :].astype(BF)
        copies[2].wait()
        out[2 * ff_cut :, :] = near_d[...]

    def stage_kernel(ids, *refs):
        qkv, gain_block = refs[chips:]
        for k in range(chips):
            if k > 0:
                qkv[(k - 1) * qkv_cut : k * qkv_cut, :] = refs[k][:qkv_cut, :]
            gain_block[k * 16 : (k + 1) * 16, :] = refs[k][qkv_cut:, :128]

    def owner_rows(ids, row):
        k, r = row % chips, row // chips
        return (ids[1] ^ k) * 2 + (ids[2] ^ r)

    def gains_kernel(ids, near, far, wide_e, wide_s, thin_e, thin_s, *outs):
        near, far = near[...].astype(F32), far[...].astype(F32)
        lane_rows = lax.broadcasted_iota(jnp.int32, (shards, 1), 0)
        owner = jnp.zeros((shards, 1), jnp.int32)
        for row in range(shards):
            owner = jnp.where(lane_rows == row, owner_rows(ids, row), owner)
        for g, out in enumerate(outs):
            block = jnp.concatenate(
                [
                    part[k * 16 + g : k * 16 + g + 1, :]
                    for part in (near, far)
                    for k in range(chips)
                ],
                axis=0,
            ).astype(BF)
            expand, seg = (wide_e, wide_s) if gain_cuts[g] == gain_cuts[0] else (thin_e, thin_s)
            spread = dot_nn(block, expand[...])
            out[...] = jnp.sum(jnp.where(seg[...] == owner, spread, 0.0), axis=0, keepdims=True)

    def attend_kernel(ids, *refs):
        toks = refs[: 2 * chips]
        packs = refs[2 * chips : 2 * chips + 2 * cols]
        wholes = refs[2 * chips + 2 * cols :][:2]
        refs = refs[2:]
        gain_attn, gain_q, gain_k, cos_ref, sin_ref = refs[2 * chips + 2 * cols :][:5]
        (xn_out, wq, wkv, q_out, k_all, v_all, q_raw_out, k_raw_out, p_out, att_out, xn_all) = refs[
            2 * chips + 2 * cols + 5 :
        ]
        me = shard_of(ids, 0, 0)
        for r in range(2):
            owner = shard_of(ids, r, 0)
            wq[pl.ds(aligned(owner, q_own), q_own), :] = wholes[r][:q_own, :]
            wkv[pl.ds(aligned(owner, kv_own), kv_own), :] = wholes[r][q_own:, :]
            for m in range(cols):
                pack = packs[r * cols + m]
                for k in range(1, chips):
                    base = shard_of(ids, r, k) * cols + (ids[0] ^ m)
                    at = (k - 1) * qkv_cut
                    wq[pl.ds(aligned(base, q_cut), q_cut), :] = pack[at : at + q_cut, :]
                    wkv[pl.ds(aligned(base, kv_cut), kv_cut), :] = pack[
                        at + q_cut : at + qkv_cut, :
                    ]
        for r in range(2):
            for k in range(chips):
                tok = toks[r * chips + k][...].astype(F32)
                normed = (tok * rms_inv(tok) * gain_attn[...]).astype(BF)
                xn_all[pl.ds(aligned(shard_of(ids, r, k), rows), rows), :] = normed
                if r == 0 and k == 0:
                    xn_out[...] = normed

        def keys_chunk(i, carry):
            at = pl.ds(aligned(i, 2 * rows), 2 * rows)
            kv = contract_cols(xn_all[at, :], wkv[...])
            key = kv[:, :hd]
            key = key * rms_inv(key) * gain_k[...]
            k_all[at, :] = spin(key, cos_ref[at, :], sin_ref[at, :]).astype(BF)
            v_all[at, :] = kv[:, hd:].astype(BF)
            return carry

        lax.fori_loop(0, chips, keys_chunk, 0)
        own = pl.ds(aligned(me, rows), rows)
        x_own = xn_out[...]
        k_raw_out[...] = contract_cols(x_own, wkv[:hd, :])
        q_raw_out[...] = contract_cols(x_own, wq[...])
        cosine, sine = cos_ref[own, :], sin_ref[own, :]
        query_pos = me * rows + lax.broadcasted_iota(jnp.int32, (rows, length), 0)
        allowed = query_pos >= lax.broadcasted_iota(jnp.int32, (rows, length), 1)
        for n in range(heads):
            raw = q_raw_out[:, n * hd : (n + 1) * hd]
            query = spin(raw * rms_inv(raw) * gain_q[...], cosine, sine).astype(BF)
            q_out[n * rows : (n + 1) * rows, :] = query
            scores = contract_cols(query, k_all[...]) * score_scale
            scores = jnp.where(allowed, scores, -1e30)
            expo = jnp.exp(scores - jnp.max(scores, axis=-1, keepdims=True))
            probs = (expo / jnp.sum(expo, axis=-1, keepdims=True)).astype(BF)
            p_out[n * rows : (n + 1) * rows, :] = probs
            att_out[:, n * hd : (n + 1) * hd] = dot_nn(probs, v_all[...]).astype(BF)

    def out_kernel(ids, att, tok, gain_pa, gain_f, *refs):
        packs = refs[: 2 * cols]
        wholes = refs[2 * cols : 2 * cols + 2]
        wo, raw_out, mid_out, xm_out = refs[2 * cols + 2 :]
        for r in range(2):
            wo[pl.ds(aligned(shard_of(ids, r, 0), q_own), q_own), :] = wholes[r][...]
            for m in range(cols):
                for k in range(1, chips):
                    base = shard_of(ids, r, k) * cols + (ids[0] ^ m)
                    wo[pl.ds(aligned(base, q_cut), q_cut), :] = packs[r * cols + m][
                        (k - 1) * q_cut : k * q_cut, :
                    ]
        raw = dot_nn(att[...], wo[...])
        raw_out[...] = raw
        mid = tok[...].astype(F32) + raw * rms_inv(raw) * gain_pa[...]
        mid_out[...] = mid
        xm_out[...] = (mid * rms_inv(mid) * gain_f[...]).astype(BF)

    def ffn_kernel(ids, *refs):
        xs = refs[:cols]
        packs = refs[cols : cols + shards]
        outs = refs[cols + shards :]
        wg, wu, wd, hid, mul_g, mul_u = outs[:6]
        parts = outs[6:]
        for j in range(shards):
            to = slice(j * ff_cut, (j + 1) * ff_cut)
            wg[to, :] = packs[j][:ff_cut, :]
            wu[to, :] = packs[j][ff_cut : 2 * ff_cut, :]
            wd[to, :] = packs[j][2 * ff_cut :, :]
        for m in range(cols):
            at = slice(m * rows, (m + 1) * rows)
            gate = contract_cols(xs[m][...], wg[...])
            up = contract_cols(xs[m][...], wu[...])
            value, slope = gelu_parts(gate)
            hidden = (value * up).astype(BF)
            parts[m][...] = dot_nn(hidden, wd[...]).astype(parts[m].dtype)
            hid[at, :] = hidden
            mul_g[at, :] = up * slope
            mul_u[at, :] = value

    def head_out_kernel(ids, *refs):
        parts = refs[:cols]
        mid, cot, gain_pf, out, gf_out, gpf_out = refs[cols:]
        raw = parts[0][...]
        for m in range(1, cols):
            raw = raw + parts[m][...].astype(F32)
        out[...] = mid[...] + raw * rms_inv(raw) * gain_pf[...]
        grad, grad_gain = norm_back_rows(cot[...], raw, gain_pf[...])
        gf_out[...] = grad.astype(BF)
        gpf_out[...] = grad_gain

    def ffn_back_kernel(ids, *refs):
        gfs = refs[:cols]
        wg, wu, wd, mul_g, mul_u = refs[cols : cols + 5]
        dg, du = refs[cols + 5 : cols + 7]
        parts = refs[cols + 7 :]
        for m in range(cols):
            at = slice(m * rows, (m + 1) * rows)
            back = contract_cols(gfs[m][...], wd[...])
            grad_g = (back * mul_g[at, :]).astype(BF)
            grad_u = (back * mul_u[at, :]).astype(BF)
            dg[at, :] = grad_g
            du[at, :] = grad_u
            part = dot_nn(grad_g, wg[...]) + dot_nn(grad_u, wu[...])
            parts[m][...] = part.astype(parts[m].dtype)

    def ffn_grads_kernel(ids, *refs):
        xs = refs[:cols]
        gfs = refs[cols : 2 * cols]
        hid, dg, du = refs[2 * cols : 2 * cols + 3]
        keep, send = refs[2 * cols + 3 : 2 * cols + 5]
        stack = refs[2 * cols + 5]
        for part, left, right in ((0, dg, xs), (1, du, xs), (2, hid, gfs)):
            for m in range(cols):
                stack[m * rows : (m + 1) * rows, :] = right[m][...]
            grad = contract_rows(left[...], stack[...])
            for k in range(chips):
                keep[k, part * ff_cut : (part + 1) * ff_cut, :] = grad[
                    k * ff_cut : (k + 1) * ff_cut, :
                ].astype(keep.dtype)
                send[k, part * ff_cut : (part + 1) * ff_cut, :] = grad[
                    (chips + k) * ff_cut : (chips + k + 1) * ff_cut, :
                ].astype(send.dtype)

    def mid_back_kernel(ids, *refs):
        parts = refs[:cols]
        mid, cot, attn_raw, gain_f, gain_pa = refs[cols : cols + 5]
        gmid_out, gab_out, gf_gain, gpa_gain = refs[cols + 5 :]
        total = parts[0][...]
        for m in range(1, cols):
            total = total + parts[m][...].astype(F32)
        grad, gain_grad = norm_back_rows(total, mid[...], gain_f[...])
        gf_gain[...] = gain_grad
        gmid = cot[...] + grad
        gmid_out[...] = gmid
        grad, gain_grad = norm_back_rows(gmid, attn_raw[...], gain_pa[...])
        gpa_gain[...] = gain_grad
        gab_out[...] = grad.astype(BF)

    def attend_back_kernel(ids, *refs):
        (gab, gain_q, wo, att, probs, q_rot, q_raw, k_all, v_all, cos_ref, sin_ref) = refs[:11]
        qgb_out, keep, send, gq_gain = refs[11:15]
        dot_b, ds, dkv = refs[15:]
        me = shard_of(ids, 0, 0)
        own = pl.ds(aligned(me, rows), rows)
        cosine, sine = cos_ref[own, :], sin_ref[own, :]
        gq_total = jnp.zeros((1, hd), F32)
        for n in range(heads):
            lanes = slice(n * hd, (n + 1) * hd)
            at = slice(n * rows, (n + 1) * rows)
            d_out = contract_cols(gab[...], wo[lanes, :]).astype(BF)
            dot_b[at, :] = d_out
            delta = jnp.sum(
                d_out.astype(F32) * att[:, lanes].astype(F32), axis=-1, keepdims=True
            )
            prob_grad = contract_cols(d_out, v_all[...])
            score_grad = (probs[at, :].astype(F32) * (prob_grad - delta)).astype(BF)
            ds[at, :] = score_grad
            q_grad = dot_nn(score_grad, k_all[...]) * score_scale
            q_grad, gain_grad = norm_back_rows(
                spin(q_grad, cosine, -sine), q_raw[:, lanes], gain_q[...]
            )
            gq_total = gq_total + gain_grad
            qgb_out[:, lanes] = q_grad.astype(BF)
        gq_gain[...] = gq_total
        dkv[:, :hd] = contract_rows(ds[...], q_rot[...]) * score_scale
        dkv[:, hd:] = contract_rows(probs[...], dot_b[...])
        for k in range(chips):
            at = pl.ds(aligned(shard_of(ids, 0, k), rows), rows)
            keep[k] = dkv[at, :].astype(BF)
            at = pl.ds(aligned(shard_of(ids, 1, k), rows), rows)
            send[k] = dkv[at, :].astype(BF)

    def pair_kernel(ids, keep, got, stay, away):
        for k in range(chips):
            dest = (stay, away)[k % 2]
            dest[k // 2] = (keep[k].astype(F32) + got[k].astype(F32)).astype(dest.dtype)

    def halve_kernel(ids, stay, got, mine, away):
        mine[...] = stay[0] + got[0].astype(F32)
        away[...] = (stay[1] + got[1].astype(F32)).astype(BF)

    def add_kernel(ids, mine, got, out):
        out[...] = (mine[...] + got[...].astype(F32)).astype(BF)

    def proj_grads_kernel(ids, qgb, xn, att, gab, wq, dx, keep, send, gq, go):
        dx[...] = dot_nn(qgb[...], wq[...])
        gq[...] = contract_rows(qgb[...], xn[...])
        go[...] = contract_rows(att[...], gab[...])
        for r, dest in ((0, keep), (1, send)):
            for m in range(cols):
                for k in range(chips):
                    base = shard_of(ids, r, k) * cols + (ids[0] ^ m)
                    at = pl.ds(aligned(base, q_cut), q_cut)
                    dest[m, k * qo_cut : k * qo_cut + q_cut, :] = gq[at, :].astype(BF)
                    dest[m, k * qo_cut + q_cut : (k + 1) * qo_cut, :] = go[at, :].astype(BF)

    def split_kernel(ids, keep, got, *outs):
        for m in range(cols):
            outs[m][...] = (keep[m].astype(F32) + got[m].astype(F32)).astype(outs[m].dtype)

    def key_back_kernel(ids, *refs):
        near, far, k_raw, gain_k, wkv, dxq, tok, gain_attn, gmid, cos_ref, sin_ref = refs[:11]
        g_q, g_pa, g_f, g_pf, wide_e, wide_s, thin_e, thin_s = refs[11:19]
        qos = refs[19 : 19 + cols]
        msgs = refs[19 + cols : 19 + cols + chips]
        gin_out, hold, grads = refs[19 + cols + chips :]
        me = shard_of(ids, 0, 0)
        own = pl.ds(aligned(me, rows), rows)
        total = near[...] + far[...].astype(F32)
        grad, g_k = norm_back_rows(
            spin(total[:, :hd], cos_ref[own, :], -sin_ref[own, :]), k_raw[...], gain_k[...]
        )
        kvb = jnp.concatenate([grad, total[:, hd:]], axis=-1).astype(BF)
        dx = dxq[...] + dot_nn(kvb, wkv[...])
        grad, g_a = norm_back_rows(dx, tok[...].astype(F32), gain_attn[...])
        gin_out[...] = gmid[...] + grad
        pair = 2 * kv_own
        for k in range(chips):
            hold[k] = kvb[:, k * pair : (k + 1) * pair]
        segment = lax.broadcasted_iota(jnp.int32, (shards, 1), 0)
        grads[...] = jnp.zeros(grads.shape, F32)
        for g, vec in enumerate((g_a, g_q[...], g_k, g_pa[...], g_f[...], g_pf[...])):
            expand, seg = (wide_e, wide_s) if gain_cuts[g] == gain_cuts[0] else (thin_e, thin_s)
            spread = jnp.where(seg[...] == segment, vec, 0.0).astype(BF)
            packed = contract_cols(spread, expand[...])
            for s in range(shards):
                grads[s, g : g + 1, :] = packed[s : s + 1, :]
        for k in range(chips):
            to = ids[1] ^ k
            msgs[k][:rows, :] = hold[to]
            msgs[k][rows : rows + 16, :] = jnp.concatenate(
                [grads[2 * to], grads[2 * to + 1]], axis=0
            ).astype(BF)
            mine = slice(k * qo_cut, (k + 1) * qo_cut)
            piece = qos[0][mine, :].astype(F32)
            for m in range(1, cols):
                piece = piece + qos[m][mine, :].astype(F32)
            piece = piece.astype(BF)
            for i in range(dim // 128):
                at = rows + 16 + i * qo_cut
                msgs[k][at : at + qo_cut, :] = piece[:, i * 128 : (i + 1) * 128]

    def last_grads_kernel(ids, *refs):
        msgs = refs[:shards]
        xn_all, out, cat, turned = refs[shards:]
        gain = jnp.zeros((16, 128), F32)
        for r in range(2):
            for k in range(chips):
                msg = msgs[r * chips + k]
                at = pl.ds(aligned(shard_of(ids, r, k), rows), rows)
                cat[at, :] = msg[:rows, :]
                gain = gain + msg[rows : rows + 16, :].astype(F32)
        turned[...] = contract_rows(cat[...], xn_all[...])
        for i in range(dim // 128):
            at = rows + 16 + i * qo_cut
            piece = msgs[0][at : at + qo_cut, :].astype(F32)
            for k in range(1, chips):
                piece = piece + msgs[k][at : at + qo_cut, :].astype(F32)
            out[:qo_cut, i * 128 : (i + 1) * 128] = piece.astype(BF)
        at = pl.ds(aligned(ids[2], kv_own), kv_own)
        out[qo_cut : qo_cut + kv_own, :] = turned[at, :].astype(BF)
        gain = jnp.where(ids[2] == 0, gain[:8, :], gain[8:, :])
        out[qo_cut + kv_own :, :] = jnp.zeros((16, dim), BF)
        out[qo_cut + kv_own :, :128] = jnp.concatenate(
            [gain, jnp.zeros((8, 128), F32)], axis=0
        ).astype(BF)

    def finish_kernel(ids, *refs):
        pieces = refs[:cols]
        out_q, out_o, out_kv = refs[cols : cols + 3]
        out_gains, hold_q = refs[cols + 3 : -1], refs[-1]
        total = pieces[0][qo_cut:, :].astype(F32)
        for m in range(1, cols):
            total = total + pieces[m][qo_cut:, :].astype(F32)
        for m in range(cols):
            at = pl.ds(aligned(ids[0] ^ m, q_cut), q_cut)
            hold_q[at, :] = pieces[m][:q_cut, :].astype(F32)
            out_o[at, :] = pieces[m][q_cut:qo_cut, :].astype(F32)
        out_q[...] = hold_q[...].T
        out_kv[...] = total[:kv_own, :]
        for g, (out, cut) in enumerate(zip(out_gains, gain_cuts)):
            out[...] = total[kv_own + g : kv_own + g + 1, :cut].reshape(cut)

    def place_kernel(spec, ids, *refs):
        pieces = refs[:cols]
        outs = refs[cols : cols + len(spec)]
        holds = refs[cols + len(spec) :]
        start = 0
        for (cut, turned), out, hold in zip(spec, outs, holds):
            for m in range(cols):
                hold[pl.ds(aligned(ids[0] ^ m, cut), cut), :] = pieces[m][
                    start : start + cut, :
                ].astype(F32)
            out[...] = hold[...].T if turned else hold[...]
            start += cut

    def place(ids, pieces, spec):
        outs = [
            ((dim, cut * cols) if turned else (cut * cols, dim), F32) for cut, turned in spec
        ]
        scratch = [pltpu.VMEM((cut * cols, dim), F32) for cut, _ in spec]
        return run_block(functools.partial(place_kernel, spec), outs, ids, *pieces, scratch=scratch)

    def both(x, y):
        return lax.optimization_barrier((x, y))

    def fast_body(
        tokens,
        attn_norm,
        query_norm,
        key_norm,
        post_attn_norm,
        ffn_norm,
        post_ffn_norm,
        query_weight,
        keyval_weight,
        out_weight,
        gate_weight,
        up_weight,
        down_weight,
        cotangent,
    ):
        me_h = lax.axis_index("head").astype(jnp.int32)
        me_s = lax.axis_index("shard").astype(jnp.int32)
        ids = jnp.stack([me_h, me_s // 2, me_s % 2])
        tok, cot = tokens[0], cotangent[0]

        pack_qkv, own_qkv = run_block(
            pack_qkv_kernel,
            [((qkv_cut + 16, dim), BF), ((q_own + kv_own, dim), BF)],
            ids,
            query_weight,
            keyval_weight.T,
            attn_norm,
            query_norm,
            key_norm,
            post_attn_norm,
            ffn_norm,
            post_ffn_norm,
            scratch=[pltpu.VMEM((dim, q_own), BF), pltpu.VMEM((kv_own, dim), BF)]
            + [pltpu.VMEM((cut,), BF) for cut in gain_cuts]
            + [
                pltpu.VMEM((q_own, dim), F32),
                pltpu.VMEM((kv_own, dim), F32),
                pltpu.VMEM((16, 128), F32),
                pltpu.SemaphoreType.DMA((2 + len(gain_cuts),)),
            ],
            space=pltpu.HBM,
            slack=56,
        )
        pack_out = lax.dynamic_slice_in_dim(out_weight, me_h * q_cut, q_cut, 0)
        (pack_ffn,) = run_block(
            pack_ffn_kernel,
            [((3 * ff_cut, dim), BF)],
            ids,
            gate_weight,
            up_weight,
            down_weight,
            scratch=[
                pltpu.VMEM((dim, ff_own), BF),
                pltpu.VMEM((dim, ff_own), BF),
                pltpu.VMEM((ff_cut, dim), BF),
                pltpu.VMEM((ff_own, dim), F32),
                pltpu.SemaphoreType.DMA((3,)),
            ],
            space=pltpu.HBM,
        )
        qkv_z = all_along(pack_qkv)
        tok_z = all_along(tok)
        out_z = all_along(pack_out)
        qkv_z, gain_block = run_block(
            stage_kernel,
            [(((chips - 1) * qkv_cut, dim), BF), ((chips * 16, 128), BF)],
            ids,
            *qkv_z,
        )
        qkv_h = with_partner(all_across(qkv_z))
        toks = with_partner(tok_z)
        out_z = jnp.concatenate(out_z[1:], axis=0)

        def spread_tables(width):
            cut = width // shards
            lane = jnp.arange(width, dtype=jnp.int32)[None, :]
            within = jnp.arange(128, dtype=jnp.int32)[:, None]
            return (lane % cut == within).astype(BF), lane // cut

        wide_e, wide_s = spread_tables(dim)
        thin_e, thin_s = spread_tables(hd)
        gain_far = swap(gain_block)
        gain_attn, gain_q, gain_k, gain_pa, gain_f, gain_pf = run_block(
            gains_kernel,
            [((1, cut * shards), F32) for cut in gain_cuts],
            ids,
            gain_block,
            gain_far,
            wide_e,
            wide_s,
            thin_e,
            thin_s,
        )
        out_h = all_across(out_z)
        ffn_z = all_along(pack_ffn)

        half = hd // 2
        freqs = jnp.exp(
            jnp.arange(half, dtype=F32) * (-2.0 * math.log(rope_base) / hd)
        )
        angles = jnp.arange(length, dtype=jnp.int32).astype(F32)[:, None] * freqs
        cos_all, sin_all = jnp.cos(angles), jnp.sin(angles)

        xn, wq, wkv, q_rot, k_all, v_all, q_raw, k_raw, probs, att, xn_all = run_block(
            attend_kernel,
            [
                ((rows, dim), BF),
                ((q_all, dim), BF),
                ((kv_all, dim), BF),
                ((heads * rows, hd), BF),
                ((length, hd), BF),
                ((length, hd), BF),
                ((rows, q_all), F32),
                ((rows, hd), F32),
                ((heads * rows, length), BF),
                ((rows, q_all), BF),
                ((length, dim), BF),
            ],
            ids,
            *toks,
            *qkv_h,
            own_qkv,
            swap(own_qkv),
            gain_attn,
            gain_q,
            gain_k,
            cos_all,
            sin_all,
        )
        att, out_h = both(att, out_h)
        out_h = with_partner(out_h)
        wo, attn_raw, mid, xm = run_block(
            out_kernel,
            [((q_all, dim), BF), ((rows, dim), F32), ((rows, dim), F32), ((rows, dim), BF)],
            ids,
            att,
            tok,
            gain_pa,
            gain_f,
            *out_h,
            out_weight,
            swap(out_weight),
        )
        xs = all_across(xm)
        ffn_z, _ = both(ffn_z, xm)
        ffn_packs = with_partner(ffn_z)
        ff_w = ((ff_local, dim), BF)
        part_outs = [((rows, dim), F32)] + [((rows, dim), BF)] * (cols - 1)
        wg, wu, wd, hid, mul_g, mul_u, *parts = run_block(
            ffn_kernel,
            [ff_w, ff_w, ff_w, ((cols * rows, ff_local), BF)]
            + [((cols * rows, ff_local), F32)] * 2
            + part_outs,
            ids,
            *xs,
            *ffn_packs,
        )
        parts = trade_across(parts)
        out, gf, g_pf = run_block(
            head_out_kernel,
            [((rows, dim), F32), ((rows, dim), BF), ((1, dim), F32)],
            ids,
            *parts,
            mid,
            cot,
            gain_pf,
        )
        gfs = all_across(gf)
        dg, du, *parts = run_block(
            ffn_back_kernel,
            [((cols * rows, ff_local), BF)] * 2 + part_outs,
            ids,
            *gfs,
            wg,
            wu,
            wd,
            mul_g,
            mul_u,
        )
        parts = trade_across(parts)
        keep, send = run_block(
            ffn_grads_kernel,
            [((chips, 3 * ff_cut, dim), BF), ((chips, 3 * ff_cut, dim), BF)],
            ids,
            *xs,
            *gfs,
            hid,
            dg,
            du,
            scratch=[pltpu.VMEM((cols * rows, dim), BF)],
        )
        parts, send = both(parts, send)
        got = swap(send)
        gmid, gab, g_f, g_pa = run_block(
            mid_back_kernel,
            [((rows, dim), F32), ((rows, dim), BF), ((1, dim), F32), ((1, dim), F32)],
            ids,
            *parts,
            mid,
            cot,
            attn_raw,
            gain_f,
            gain_pa,
        )
        ff_piece = (3 * ff_cut, dim)
        ff_stay, ff_away = run_block(
            pair_kernel, [((2,) + ff_piece, F32), ((2,) + ff_piece, BF)], ids, keep, got
        )
        ff_got = along(ff_away, 1)

        qgb, keep, send, g_q = run_block(
            attend_back_kernel,
            [
                ((rows, q_all), BF),
                ((chips, rows, kv_all), BF),
                ((chips, rows, kv_all), BF),
                ((1, hd), F32),
            ],
            ids,
            gab,
            gain_q,
            wo,
            att,
            probs,
            q_rot,
            q_raw,
            k_all,
            v_all,
            cos_all,
            sin_all,
            scratch=[
                pltpu.VMEM((heads * rows, hd), BF),
                pltpu.VMEM((heads * rows, length), BF),
                pltpu.VMEM((length, kv_all), F32),
            ],
        )
        got = swap(send)
        kv_piece = (rows, kv_all)
        kv_stay, kv_away = run_block(
            pair_kernel, [((2,) + kv_piece, F32), ((2,) + kv_piece, BF)], ids, keep, got
        )
        kv_got = along(kv_away, 1)
        dxq, keep, send = run_block(
            proj_grads_kernel,
            [
                ((rows, dim), F32),
                ((cols, chips * qo_cut, dim), BF),
                ((cols, chips * qo_cut, dim), BF),
            ],
            ids,
            qgb,
            xn,
            att,
            gab,
            wq,
            scratch=[pltpu.VMEM((q_all, dim), F32)] * 2,
        )
        got = swap(send)
        ff_mine, ff_away = run_block(
            halve_kernel, [(ff_piece, F32), (ff_piece, BF)], ids, ff_stay, ff_got
        )
        ff_got = along(ff_away, 2)
        kv_mine, kv_away = run_block(
            halve_kernel, [(kv_piece, F32), (kv_piece, BF)], ids, kv_stay, kv_got
        )
        kv_got = along(kv_away, 2)
        qo_parts = run_block(split_kernel, [((chips * qo_cut, dim), BF)] * cols, ids, keep, got)
        qo_parts = trade_across(qo_parts)
        *msgs, grad_input = run_block(
            key_back_kernel,
            [((rows + 16 + qo_cut * dim // 128, 2 * kv_own), BF)] * chips + [((rows, dim), F32)],
            ids,
            kv_mine,
            kv_got,
            k_raw,
            gain_k,
            wkv,
            dxq,
            tok,
            gain_attn,
            gmid,
            cos_all,
            sin_all,
            g_q,
            g_pa,
            g_f,
            g_pf,
            wide_e,
            wide_s,
            thin_e,
            thin_s,
            *qo_parts,
            scratch=[pltpu.VMEM((chips, rows, 2 * kv_own), BF), pltpu.VMEM((shards, 8, 128), F32)],
        )
        msgs = trade_along(msgs)
        (ff_sum,) = run_block(add_kernel, [(ff_piece, BF)], ids, ff_mine, ff_got)
        ff_pieces = all_across(ff_sum)
        msgs = with_partner(msgs)
        last = (qo_cut + kv_own + 16, dim)
        (piece,) = run_block(
            last_grads_kernel,
            [(last, BF)],
            ids,
            *msgs,
            xn_all,
            scratch=[pltpu.VMEM((length, 2 * kv_own), BF), pltpu.VMEM((2 * kv_own, dim), F32)],
        )
        pieces = all_across(piece)
        ff_pieces, _ = both(ff_pieces, piece)
        grad_gate, grad_up, grad_down = place(
            ids, ff_pieces, ((ff_cut, True), (ff_cut, True), (ff_cut, False))
        )
        grad_query_w, grad_out, grad_keyval_w, *small = run_block(
            finish_kernel,
            [
                ((dim, q_own), F32),
                ((q_own, dim), F32),
                ((kv_own, dim), F32),
            ]
            + [((cut,), F32) for cut in gain_cuts],
            ids,
            *pieces,
            scratch=[pltpu.VMEM((q_own, dim), F32)],
        )
        grad_keyval_w = grad_keyval_w.T
        return (
            out[None],
            grad_input[None],
            *small,
            grad_query_w,
            grad_keyval_w,
            grad_out,
            grad_gate,
            grad_up,
            grad_down,
        )

    return fast_body


def power_of_two(number):
    return number & (number - 1) == 0


def direct_fits(mesh, tokens, query_weight, keyval_weight, gate_weight):
    cols, shards = mesh.shape["head"], mesh.shape["shard"]
    parts = cols * shards
    return (
        power_of_two(cols)
        and power_of_two(shards)
        and cols <= 4
        and 2 <= shards <= 8
        and tokens.shape[1] <= 1024
        and tokens.shape[2] % 128 == 0
        and tokens.shape[1] % (16 * shards) == 0
        and keyval_weight.shape[1] % 512 == 0
        and tokens.shape[2] <= 128 * shards
        and keyval_weight.shape[1] == 64 * shards
        and all(w.shape[1] % (16 * parts) == 0 for w in (query_weight, keyval_weight, gate_weight))
    )


def solution(mesh):
    placed = (
        P("head", "shard", None),
        P("shard"),
        P("shard"),
        P("shard"),
        P("shard"),
        P("shard"),
        P("shard"),
        P(None, "shard"),
        P(None, "shard"),
        P("shard", None),
        P(None, "shard"),
        P(None, "shard"),
        P("shard", None),
        P("head", "shard", None),
    )

    def run(*args):
        tokens, query_weight, keyval_weight, gate_weight = args[0], args[7], args[8], args[10]
        inner = body
        if direct_fits(mesh, tokens, query_weight, keyval_weight, gate_weight):
            widths = (query_weight.shape[1], keyval_weight.shape[1], gate_weight.shape[1])
            inner = make_fast(mesh, tokens.shape, widths)
        return jax.shard_map(
            inner,
            mesh=mesh,
            in_specs=placed,
            out_specs=(
                P("head", "shard", None),
                P("head", "shard", None),
                P("shard"),
                P("shard"),
                P("shard"),
                P("shard"),
                P("shard"),
                P("shard"),
                P(None, "shard"),
                P(None, "shard"),
                P("shard", None),
                P(None, "shard"),
                P(None, "shard"),
                P("shard", None),
            ),
            check_vma=False,
        )(*args)

    return run
```
